32 devices in a mesh: dp: 2 (over x), expert: 16 (over z, y, core).
Axes of the slice: x: 2, y: 2, z: 4, core: 2. Of those that a mesh axis runs over, the one named last changes fastest.
Arguments:
- tokens: bfloat16 [2048, 2048], P('expert'), may hold values from -6 to 6
- routing: int32 [2048, 8], P('expert'), may hold values from 0 to 31, all different within a row; in each aligned block of 128 rows (0 to 127, 128 to 255, ...) at most 48 rows name the same one
- route_gates: float32 [2048, 8], P('expert'), may hold values from 0.03 to 0.3
- gate_weight: bfloat16 [32, 2048, 768], P('expert', None, 'dp'), may hold values from -0.125 to 0.125
- up_weight: bfloat16 [32, 2048, 768], P('expert', None, 'dp'), may hold values from -0.125 to 0.125
- down_weight: bfloat16 [32, 2048, 768], P('expert', None, 'dp'), may hold values from -0.21875 to 0.21875
- cotangent: bfloat16 [2048, 2048], P('expert'), may hold values from -4 to 4
Outputs:
- mixed: bfloat16 [2048, 2048], P('expert', 'dp')
- token_grad: bfloat16 [2048, 2048], P('expert', 'dp')
- gates_grad: float32 [2048, 8], P('expert')
- gate_grad: bfloat16 [32, 2048, 768], P('expert', None, 'dp')
- up_grad: bfloat16 [32, 2048, 768], P('expert', None, 'dp')
- down_grad: bfloat16 [32, 2048, 768], P('expert', None, 'dp')
The draws below stay inside these ranges and needn't reach their ends.
Inputs may be any that keep to these rules, and one draw needn't show every extreme that they name: `routing`: each row names 8 different experts. Among the rows of one index of expert (aligned blocks of 128 rows) no expert is named more than 48 times, a bound that some block reaches.
All inputs are finite; a program needn't handle non-finite values.
Results may differ from the reference program's by a relative error of at most 0.012.
Values may be sent and summed in bfloat16 or wider, within the bound.
A program may use at most 192 MiB of HBM per device.

```python
import math
import jax
import jax.numpy as jnp
import numpy as np
from jax import lax

D = 2048
FF = 768
TOPK = 8
TOK_DEV = 128
EXPERTS = 32
TOKENS = 2048
CAP = 48
N_EXPERT = 16


def steps_of(rng, shape, cuts, smallest, high):
    factor_of = 1.0
    for dim, shards_of in cuts:
        steps = jax.random.uniform(jax.random.fold_in(jax.random.fold_in(rng, 6), dim), (shards_of,), jnp.float32, smallest / len(cuts), high / len(cuts))
        factor_of = factor_of * jnp.repeat(jnp.exp(steps), shape[dim] // shards_of).reshape((-1,) + (1,) * (len(shape) - 1 - dim))
    return factor_of


def deal_out(key, own, number, rows, number_of, top, most, lean):
    sequence = jax.random.permutation(key, number_of)
    crowded, common = shares(number_of, rows * top, most, lean, True), shares(number_of, rows * top, most, lean, False)
    places = jnp.arange(number_of)

    def named(tallies, rotation):
        used = int((tallies > 0).sum())
        fixed = max(1, used // 4)
        moved = fixed + (places - fixed + rotation * (used - fixed)) % max(1, number_of - fixed)
        return jnp.zeros((number_of,), jnp.int32).at[sequence[jnp.where(places < fixed, places, moved)]].set(jnp.asarray(tallies, jnp.int32))

    tallies = jnp.where(number % 4 == 0, named(crowded, number // 4), named(common, number - number // 4 - 1))
    mixed = jax.random.permutation(jax.random.fold_in(own, 3), number_of)
    source_of, taker = mixed[0:number_of // 2 * 2:2], mixed[1:number_of // 2 * 2:2]
    room = jnp.minimum(tallies[source_of] - 1, most - tallies[taker]) // 2
    room = jnp.where((source_of == sequence[0]) | (taker == sequence[0]) | (tallies[taker] == 0), 0, jnp.maximum(room, 0))
    moved = jax.random.randint(jax.random.fold_in(own, 4), (number_of // 2,), 0, 1 << 20) % (room + 1)
    tallies = tallies.at[source_of].add(-moved).at[taker].add(moved)
    members = jnp.searchsorted(jnp.cumsum(tallies), jnp.arange(rows * top), side="right").astype(jnp.int32)
    grid = members.reshape(top, rows).T
    grid = grid[jax.random.permutation(jax.random.fold_in(own, 1), rows)]
    rotation = jax.random.randint(jax.random.fold_in(own, 2), (rows, 1), 0, top)
    return jnp.take_along_axis(grid, (jnp.arange(top)[None, :] + rotation) % top, axis=1)


def shares(count, total, limit, skew, full):
    weights = [(1 << 20) // math.isqrt(grade ** skew) + 1 for grade in range(1, count + 1)]
    largest = limit if full else min(limit, max(-(-total // count), total * weights[0] // sum(weights)))
    least = 1 if total - largest >= count - 1 else 0
    holding, rest = [largest] + [least] * (count - 1), total - largest - least * (count - 1)
    while rest > 0:
        candidates = [i for i in range(1, count) if holding[i] < largest] or [i for i in range(1, count) if holding[i] < limit]
        whole, budget = sum([weights[i] for i in candidates]), rest
        for i in candidates:
            more = min(limit - holding[i], max(1, budget * weights[i] // whole), rest)
            holding[i] = holding[i] + more
            rest = rest - more
    return np.array(holding)


def centred(key, extent, scale, limit, cuts=(), kind=jnp.bfloat16):
    loudness = steps_of(key, extent, cuts, -0.22, 0.18) if cuts else 1.0
    values = jax.random.normal(key, extent, jnp.float32) * scale * loudness
    return jnp.minimum(jnp.maximum(values, -limit), limit).astype(kind)


def setup_inputs(seed: int = 0) -> dict:
    seeds = jax.random.split(jax.random.key(seed), 8)
    tokens = centred(seeds[0], (TOKENS, D), 1.0, 6.0, ((0, 16),))
    routing_keys = jax.random.split(jax.random.fold_in(seeds[1], 1), TOKENS // TOK_DEV)
    routing_turns = jax.random.permutation(jax.random.fold_in(seeds[1], 3), TOKENS // TOK_DEV)
    routing = jax.vmap(lambda own, number: deal_out(jax.random.fold_in(seeds[1], 2), own, number, TOK_DEV, EXPERTS, TOPK, CAP, 2))(routing_keys, routing_turns).reshape((TOKENS, TOPK))
    route_gates = jnp.clip(jnp.exp(math.log(0.3) - 2.3025852 * jax.random.uniform(seeds[2], (TOKENS, TOPK), jnp.float32) ** steps_of(seeds[2], (TOKENS, TOPK), ((0, 16),), -0.2, 0.2)), 0.03, 0.3)
    gate_weight = centred(seeds[3], (EXPERTS, D, FF), D ** -0.5, 0.125, ((0, 16), (2, 2)))
    up_weight = centred(seeds[4], (EXPERTS, D, FF), D ** -0.5, 0.125, ((0, 16), (2, 2)))
    down_weight = centred(seeds[5], (EXPERTS, D, FF), FF ** -0.5, 0.21875, ((0, 16), (2, 2)))
    cotangent = centred(seeds[6], (TOKENS, D), 0.5, 4.0, ((0, 16),))
    return {"tokens": tokens, "routing": routing, "route_gates": route_gates, "gate_weight": gate_weight, "up_weight": up_weight, "down_weight": down_weight, "cotangent": cotangent}


def expert_pass(slot_rows, slot_probs, slot_dout, w_gate, w_up, w_down):
    gate_pre = jnp.dot(slot_rows, w_gate, preferred_element_type=jnp.float32)
    up_pre = jnp.dot(slot_rows, w_up, preferred_element_type=jnp.float32)
    sigmoid_gate = jax.nn.sigmoid(gate_pre)
    active = gate_pre * sigmoid_gate
    hidden = (active * up_pre).astype(jnp.bfloat16)
    output = jnp.dot(hidden, w_down.T, preferred_element_type=jnp.float32).astype(jnp.bfloat16)
    slot_back = (slot_probs[:, None] * slot_dout.astype(jnp.float32)).astype(jnp.bfloat16)
    dhidden = jnp.dot(slot_back, w_down, preferred_element_type=jnp.float32)
    d_gate = (dhidden * up_pre * sigmoid_gate * (1.0 + gate_pre * (1.0 - sigmoid_gate))).astype(jnp.bfloat16)
    d_up = (dhidden * active).astype(jnp.bfloat16)
    row_grad = jnp.dot(d_gate, w_gate.T, preferred_element_type=jnp.float32)
    row_grad = (row_grad + jnp.dot(d_up, w_up.T, preferred_element_type=jnp.float32)).astype(jnp.bfloat16)
    grad_g = jnp.dot(slot_rows.T, d_gate, preferred_element_type=jnp.float32).astype(jnp.bfloat16)
    grad_u = jnp.dot(slot_rows.T, d_up, preferred_element_type=jnp.float32).astype(jnp.bfloat16)
    grad_d = jnp.dot(slot_back.T, hidden, preferred_element_type=jnp.float32).astype(jnp.bfloat16)
    return output, row_grad, grad_g, grad_u, grad_d


def reference(tokens, routing, route_gates, gate_weight, up_weight, down_weight, cotangent):
    blocks = N_EXPERT
    per_block = TOK_DEV * TOPK
    chosen = routing.reshape(blocks, per_block).astype(jnp.int32)
    one_hot = (chosen[:, :, None] == jnp.arange(EXPERTS, dtype=jnp.int32)[None, None, :]).astype(jnp.int32)
    running = jnp.cumsum(one_hot, axis=1) - one_hot
    within = jnp.sum(running * one_hot, axis=2).astype(jnp.int32)
    position = (jnp.arange(blocks, dtype=jnp.int32)[:, None] * CAP + within).astype(jnp.int32)
    assigned = jnp.arange(blocks * per_block, dtype=jnp.int32).reshape(blocks, per_block)
    table = jnp.full((EXPERTS, blocks * CAP), -1, jnp.int32).at[chosen, position].set(assigned)
    flat_gates = route_gates.reshape(-1)

    def one_expert(expert):
        ids = table[expert]
        valid = ids >= 0
        safe = jnp.maximum(ids, 0).astype(jnp.int32)
        source = (safe // TOPK).astype(jnp.int32)
        slot_rows = jnp.where(valid[:, None], tokens[source], jnp.zeros((), jnp.bfloat16))
        slot_probs = jnp.where(valid, flat_gates[safe], jnp.zeros((), jnp.float32))
        slot_dout = jnp.where(valid[:, None], cotangent[source], jnp.zeros((), jnp.bfloat16))
        return expert_pass(slot_rows, slot_probs, slot_dout,
                           gate_weight[expert], up_weight[expert], down_weight[expert])

    outputs, row_grads, gate_grad, up_grad, down_grad = lax.map(one_expert, jnp.arange(EXPERTS, dtype=jnp.int32))
    expert_rows = outputs[chosen, position].reshape(TOKENS, TOPK, D)
    grad_rows = row_grads[chosen, position].reshape(TOKENS, TOPK, D)
    expert_f = expert_rows.astype(jnp.float32)
    mixed = jnp.einsum('tk,tkd->td', route_gates, expert_f).astype(jnp.bfloat16)
    gates_grad = jnp.einsum('td,tkd->tk', cotangent.astype(jnp.float32), expert_f)
    token_grad = jnp.sum(grad_rows.astype(jnp.float32), axis=1).astype(jnp.bfloat16)
    return mixed, token_grad, gates_grad, gate_grad, up_grad, down_grad
```

```python
import functools

import jax
import jax.numpy as jnp
from jax import lax
from jax.experimental import pallas as pl
from jax.experimental.pallas import tpu as pltpu
from jax.sharding import PartitionSpec as P


def dot(a, b, dims):
    return lax.dot_general(a, b, (dims, ((), ())), preferred_element_type=jnp.float32)


def body_whole(tokens, routing, route_gates, gate_weight, up_weight, down_weight, cotangent):
    local_count = gate_weight.shape[0]
    first = lax.axis_index("expert") * local_count

    all_tokens = lax.all_gather(tokens, "expert", axis=0, tiled=True)
    picks = routing.shape[1]
    routes = jnp.concatenate([routing.astype(jnp.float32), route_gates], axis=1)
    all_routes = lax.all_gather(routes, "expert", axis=0, tiled=True)
    all_routing, all_gates = all_routes[:, :picks].astype(jnp.int32), all_routes[:, picks:]
    all_cotangent = lax.all_gather(cotangent, "expert", axis=0, tiled=True)

    named = [all_routing == first + j for j in range(local_count)]
    gate_of = [
        jnp.sum(jnp.where(named[j], all_gates, 0.0), axis=1, keepdims=True)
        for j in range(local_count)
    ]

    saved = []
    mixed_part = None
    for j in range(local_count):
        gate_pre = dot(all_tokens, gate_weight[j], ((1,), (0,)))
        up_pre = dot(all_tokens, up_weight[j], ((1,), (0,)))
        sigmoid_gate = jax.nn.sigmoid(gate_pre)
        active = gate_pre * sigmoid_gate
        hidden = active * up_pre
        weighted_hidden = (gate_of[j] * hidden).astype(jnp.bfloat16)
        saved.append((gate_pre.astype(jnp.bfloat16), up_pre.astype(jnp.bfloat16), weighted_hidden))
    hidden_cat = jnp.concatenate([s[2] for s in saved], axis=1)
    down_cat = jnp.concatenate([down_weight[j] for j in range(local_count)], axis=1)
    mixed_part = dot(hidden_cat, down_cat, ((1,), (1,))).astype(jnp.bfloat16)
    mixed_rows = lax.psum_scatter(mixed_part, "expert", scatter_dimension=0, tiled=True)

    grads = []
    gates_part = 0.0
    for j in range(local_count):
        gate_pre, up_pre, weighted_hidden = saved[j]
        gate_pre, up_pre = gate_pre.astype(jnp.float32), up_pre.astype(jnp.float32)
        raw = dot(all_cotangent, down_weight[j], ((1,), (0,)))
        sigmoid_gate = jax.nn.sigmoid(gate_pre)
        active = gate_pre * sigmoid_gate
        pair = jnp.sum(raw * (active * up_pre), axis=1, keepdims=True)
        gates_part = gates_part + jnp.where(named[j], pair, 0.0)
        dhidden = gate_of[j] * raw
        d_gate = (dhidden * up_pre * sigmoid_gate * (1.0 + gate_pre * (1.0 - sigmoid_gate))).astype(
            jnp.bfloat16
        )
        d_up = (dhidden * active).astype(jnp.bfloat16)
        grads.append((d_gate, d_up))
    d_cat = jnp.concatenate([g for pair in grads for g in pair], axis=1)
    w_cat = jnp.concatenate(
        [w for j in range(local_count) for w in (gate_weight[j], up_weight[j])], axis=1
    )
    token_part = dot(d_cat, w_cat, ((1,), (1,))).astype(jnp.bfloat16)
    token_rows = lax.psum_scatter(token_part, "expert", scatter_dimension=0, tiled=True)
    mixed = lax.psum_scatter(mixed_rows, "dp", scatter_dimension=1, tiled=True)
    token_grad = lax.psum_scatter(token_rows, "dp", scatter_dimension=1, tiled=True)
    gates_grad = lax.psum(
        lax.psum_scatter(gates_part, "expert", scatter_dimension=0, tiled=True), "dp"
    )

    grad_g = jnp.stack([dot(all_tokens, g, ((0,), (0,))).astype(jnp.bfloat16) for g, _ in grads])
    grad_u = jnp.stack([dot(all_tokens, u, ((0,), (0,))).astype(jnp.bfloat16) for _, u in grads])
    grad_d = jnp.stack(
        [dot(all_cotangent, s[2], ((0,), (0,))).astype(jnp.bfloat16) for s in saved]
    )
    return (mixed, token_grad, gates_grad, grad_g, grad_u, grad_d)


def expert_forward(slot_rows, w_gate, w_up, w_down):
    gate_pre = jnp.einsum("jrd,jdf->jrf", slot_rows, w_gate, preferred_element_type=jnp.float32)
    up_pre = jnp.einsum("jrd,jdf->jrf", slot_rows, w_up, preferred_element_type=jnp.float32)
    sigmoid_gate = jax.nn.sigmoid(gate_pre)
    active = gate_pre * sigmoid_gate
    hidden = (active * up_pre).astype(jnp.bfloat16)
    out_part = jnp.einsum("jrf,jdf->jrd", hidden, w_down, preferred_element_type=jnp.float32)
    return (out_part, (gate_pre, up_pre, sigmoid_gate, active, hidden))


def expert_backward(slot_rows, slot_back, saved, w_gate, w_up, w_down):
    gate_pre, up_pre, sigmoid_gate, active, hidden = saved
    dhidden = jnp.einsum("jrd,jdf->jrf", slot_back, w_down, preferred_element_type=jnp.float32)
    d_gate = (dhidden * up_pre * sigmoid_gate * (1.0 + gate_pre * (1.0 - sigmoid_gate))).astype(
        jnp.bfloat16
    )
    d_up = (dhidden * active).astype(jnp.bfloat16)
    row_part = jnp.einsum("jrf,jdf->jrd", d_gate, w_gate, preferred_element_type=jnp.float32)
    row_part = row_part + jnp.einsum("jrf,jdf->jrd", d_up, w_up, preferred_element_type=jnp.float32)
    grad_g = jnp.einsum("jrd,jrf->jdf", slot_rows, d_gate, preferred_element_type=jnp.float32)
    grad_u = jnp.einsum("jrd,jrf->jdf", slot_rows, d_up, preferred_element_type=jnp.float32)
    grad_d = jnp.einsum("jrd,jrf->jdf", slot_back, hidden, preferred_element_type=jnp.float32)
    return (row_part, (grad_g, grad_u, grad_d))


def body_slots(tokens, routing, route_gates, gate_weight, up_weight, down_weight, cotangent):
    rows_here, width = tokens.shape
    picks = routing.shape[1]
    local_count = gate_weight.shape[0]
    devices = lax.axis_size("expert")
    experts_all = local_count * devices
    capacity = 3 * rows_here * picks // (2 * experts_all)
    member = lax.axis_index("dp")
    chosen = routing.reshape(-1)
    one_hot = (chosen[:, None] == jnp.arange(experts_all, dtype=jnp.int32)[None, :]).astype(
        jnp.int32
    )
    running = jnp.cumsum(one_hot, axis=0) - one_hot
    within = jnp.sum(running * one_hot, axis=1)
    owners = chosen // local_count
    slots = chosen % local_count
    source_row = jnp.arange(rows_here * picks, dtype=jnp.int32) // picks
    flat_gates = route_gates.reshape(-1)
    x_rows = tokens[source_row]
    weighted = (flat_gates[:, None] * cotangent[source_row].astype(jnp.float32)).astype(
        jnp.bfloat16
    )
    half_cap = (capacity + 1) // 2
    mine = within // half_cap == member
    local_within = jnp.clip(within - member * half_cap, 0, half_cap - 1)
    target = jnp.where(mine, owners, devices)

    def scatter_share(values):
        buffer = jnp.zeros((local_count, devices, half_cap) + values.shape[1:], values.dtype)
        return buffer.at[slots, target, local_within].set(values, mode="drop")

    def gather_share(buffer):
        picked = buffer.at[slots, target, local_within].get(mode="fill", fill_value=0)
        return jnp.where(mine[:, None], picked, jnp.zeros((), picked.dtype))

    full_gate, full_up, full_down = (
        lax.all_gather(gate_weight, "dp", axis=2, tiled=True),
        lax.all_gather(up_weight, "dp", axis=2, tiled=True),
        lax.all_gather(down_weight, "dp", axis=2, tiled=True),
    )
    got_rows, got_back = (
        lax.all_to_all(scatter_share(x_rows), "expert", split_axis=1, concat_axis=1, tiled=True),
        lax.all_to_all(scatter_share(weighted), "expert", split_axis=1, concat_axis=1, tiled=True),
    )
    slot_rows = got_rows.reshape(local_count, devices * half_cap, width)
    slot_back = got_back.reshape(local_count, devices * half_cap, width)
    out_full, saved = expert_forward(slot_rows, full_gate, full_up, full_down)
    row_full, grads_full = expert_backward(
        slot_rows, slot_back, saved, full_gate, full_up, full_down
    )
    share_shape = (local_count, devices, half_cap, width)
    back_out, back_grad = (
        lax.all_to_all(
            out_full.astype(jnp.bfloat16).reshape(share_shape),
            "expert",
            split_axis=1,
            concat_axis=1,
            tiled=True,
        ),
        lax.all_to_all(
            row_full.astype(jnp.bfloat16).reshape(share_shape),
            "expert",
            split_axis=1,
            concat_axis=1,
            tiled=True,
        ),
    )
    expert_rows = gather_share(back_out).reshape(rows_here, picks, width)
    grad_rows = gather_share(back_grad).reshape(rows_here, picks, width)
    gate_part = jnp.einsum("td,tkd->tk", cotangent, expert_rows, preferred_element_type=jnp.float32)
    mixed_part = jnp.einsum("tk,tkd->td", route_gates, expert_rows.astype(jnp.float32))
    token_part = jnp.sum(grad_rows.astype(jnp.float32), axis=1)
    mixed_sum, token_sum = (
        lax.psum_scatter(
            mixed_part.astype(jnp.bfloat16), "dp", scatter_dimension=1, tiled=True
        ).astype(jnp.float32),
        lax.psum_scatter(
            token_part.astype(jnp.bfloat16), "dp", scatter_dimension=1, tiled=True
        ).astype(jnp.float32),
    )
    mixed = mixed_sum.astype(jnp.bfloat16)
    token_grad = token_sum.astype(jnp.bfloat16)
    grad_g, grad_u, grad_d = (
        lax.psum_scatter(
            grads_full[0].astype(jnp.bfloat16), "dp", scatter_dimension=2, tiled=True
        ).astype(jnp.float32),
        lax.psum_scatter(
            grads_full[1].astype(jnp.bfloat16), "dp", scatter_dimension=2, tiled=True
        ).astype(jnp.float32),
        lax.psum_scatter(
            grads_full[2].astype(jnp.bfloat16), "dp", scatter_dimension=2, tiled=True
        ).astype(jnp.float32),
    )
    grad_g = grad_g.astype(jnp.bfloat16)
    grad_u = grad_u.astype(jnp.bfloat16)
    grad_d = grad_d.astype(jnp.bfloat16)
    gates_grad = lax.psum(gate_part, "dp")
    return (mixed, token_grad, gates_grad, grad_g, grad_u, grad_d)


MESH = pl.DeviceIdType.MESH


class Place:
    def __init__(self, line):
        self.x = lax.axis_index("dp")
        self.e = lax.axis_index("expert")
        self.line = line
        self.z = self.e // 4
        self.y = (self.e // 2) % 2
        self.c = self.e % 2
        self.to_x = (1 - self.x, self.e)
        self.to_y = (self.x, self.e + 2 - 4 * self.y)
        self.to_core = (self.x, self.e + 1 - 2 * self.c)
        self.to_right = (self.x, (self.e + 4) % (4 * line))
        self.to_left = (self.x, (self.e + 4 * line - 4) % (4 * line))
        self.has_right = self.z < line - 1
        self.has_left = self.z > 0
        half = self.z // 2
        self.mate = self.z + 1 - 2 * (self.z % 2)
        self.inner = 2 - half
        self.outer = 3 - 3 * half


def greet(p):
    barrier = pltpu.get_barrier_semaphore()
    for to in (p.to_x, p.to_y, p.to_core):
        pl.semaphore_signal(barrier, inc=1, device_id=to, device_id_type=MESH)

    @pl.when(p.has_right)
    def _():
        pl.semaphore_signal(barrier, inc=1, device_id=p.to_right, device_id_type=MESH)

    @pl.when(p.has_left)
    def _():
        pl.semaphore_signal(barrier, inc=1, device_id=p.to_left, device_id_type=MESH)

    ahead = (2 * p.line - 2 - p.z) // p.line
    behind = (p.line - 1 + p.z) // p.line
    pl.semaphore_wait(barrier, 3 + ahead + behind)


class Mail:
    def __init__(self, send_sem, recv_sem):
        self.send_sem, self.recv_sem, self.sent = send_sem, recv_sem, []

    def copy(self, src, dst, slot, to, send_slot=None):
        return pltpu.make_async_remote_copy(
            src_ref=src,
            dst_ref=dst,
            send_sem=self.send_sem.at[send_slot or slot],
            recv_sem=self.recv_sem.at[slot],
            device_id=to,
            device_id_type=MESH,
        )

    def send(self, src, dst, slot, to, send_slot=None, when=None):
        copy = self.copy(src, dst, slot, to, send_slot)
        self.sent.append((copy, when))
        if when is None:
            copy.start()
        else:
            pl.when(when)(copy.start)

    def wait(self, dst, slot, to, when=None):
        copy = self.copy(dst, dst, slot, to)
        if when is None:
            copy.wait_recv()
        else:
            pl.when(when)(copy.wait_recv)

    def finish(self):
        for copy, when in self.sent:
            if when is None:
                copy.wait_send()
            else:
                pl.when(when)(copy.wait_send)
        self.sent = []


Z_IN, Y_ONE, X_TWO, X_ONE, Y_TWO, CORE, Z_LEFT = range(7)


def spread_kernel(line, tok, cot, routes, all_tok, all_cot, all_routes, send_sem, recv_sem, own_sem):
    p = Place(line)
    x, y, c, z = p.x, p.y, p.c, p.z
    own = [
        pltpu.make_async_copy(src, dst.at[z, y, c], own_sem.at[t])
        for t, (src, dst) in enumerate(((tok, all_tok), (cot, all_cot), (routes, all_routes)))
    ]
    for copy in own:
        copy.start()
    greet(p)
    mail = Mail(send_sem, recv_sem)
    pairs = ((0, tok, all_tok), (1, cot, all_cot))

    here = all_routes.at[z, y, c]
    mail.send(routes, here, (2, Z_IN, z), p.to_right, when=p.has_right)
    mail.send(routes, here, (2, Z_IN, z), p.to_left, send_slot=(2, Z_LEFT, z), when=p.has_left)
    for t, src, dst in pairs:
        piece = dst.at[z, y, c, x]
        mail.send(src.at[x], piece, (t, Y_ONE, z), p.to_y)
        mail.send(src.at[x], piece, (t, Z_IN, z), p.to_right, when=p.has_right)
        mail.send(
            src.at[x], piece, (t, Z_IN, z), p.to_left, send_slot=(t, Z_LEFT, z), when=p.has_left
        )

    for t, src, dst in pairs:
        piece = dst.at[z, 1 - y, c, x]
        mail.wait(piece, (t, Y_ONE, z), p.to_y)
        mail.send(piece, piece, (t, X_TWO, z), p.to_x)

    def routes_on(far):
        piece = all_routes.at[far, y, c]
        mail.wait(piece, (2, Z_IN, far), p.to_left)
        mail.send(piece, piece, (2, Z_IN, far), p.to_right, when=(far < z) & p.has_right)
        mail.send(
            piece, piece, (2, Z_IN, far), p.to_left, send_slot=(2, Z_LEFT, far),
            when=(far > z) & p.has_left,
        )

    def first(t, dst, far):
        piece = dst.at[far, y, c, x]
        mail.wait(piece, (t, Z_IN, far), p.to_left)
        mail.send(piece, piece, (t, Z_IN, far), p.to_right, when=(far < z) & p.has_right)
        mail.send(
            piece, piece, (t, Z_IN, far), p.to_left, send_slot=(t, Z_LEFT, far),
            when=(far > z) & p.has_left,
        )
        mail.send(piece.at[0], piece.at[0], (t, Y_ONE, far), p.to_y)
        mail.send(piece.at[1], piece.at[1], (t, X_ONE, far), p.to_x)

    def second(t, dst, far):
        mail.wait(dst.at[far, 1 - y, c, x, 0], (t, Y_ONE, far), p.to_y)
        both = dst.at[far, :, c, x, 0]
        mail.send(both, both, (t, X_TWO, far), p.to_x)
        mail.wait(dst.at[far, y, c, 1 - x, 1], (t, X_ONE, far), p.to_x)
        both = dst.at[far, y, c, :, 1]
        mail.send(both, both, (t, Y_TWO, far), p.to_y)

    def third(t, dst, far):
        mail.wait(dst.at[far, :, c, 1 - x, 0], (t, X_TWO, far), p.to_x)
        mail.wait(dst.at[far, 1 - y, c, :, 1], (t, Y_TWO, far), p.to_y)
        mail.send(dst.at[far, :, c], dst.at[far, :, c], (t, CORE, far), p.to_core)

    far_groups = (p.mate, p.inner, p.outer)
    for far in far_groups:
        routes_on(far)
        for t, _, dst in pairs:
            first(t, dst, far)
    for t, src, dst in pairs:
        own[t].wait()
        mail.wait(dst.at[z, 1 - y, c, 1 - x], (t, X_TWO, z), p.to_x)
        mail.send(dst.at[z, :, c], dst.at[z, :, c], (t, CORE, z), p.to_core)
    for far in far_groups:
        for t, _, dst in pairs:
            second(t, dst, far)
    own[2].wait()
    mail.send(all_routes.at[:, y, c], all_routes.at[:, y, c], (2, Y_ONE, 0), p.to_y)
    for far in far_groups:
        for t, _, dst in pairs:
            third(t, dst, far)
    mail.wait(all_routes.at[:, 1 - y, c], (2, Y_ONE, 0), p.to_y)
    mail.send(all_routes.at[:, :, c], all_routes.at[:, :, c], (2, CORE, 0), p.to_core)
    for far in far_groups + (z,):
        for t, _, dst in pairs:
            mail.wait(dst.at[far, :, 1 - c], (t, CORE, far), p.to_core)
    mail.wait(all_routes.at[:, :, 1 - c], (2, CORE, 0), p.to_core)
    mail.finish()


def expert_kernel(cap, tok, cot, routes, w_gate, w_up, w_down, out_part, row_part, pair_part,
                  x_rows, c_rows, d_gate, d_up, w_hidden, pick, out_rows, row_rows):
    count, width, hidden_units = w_gate.shape
    blocks = 4
    rows = tok.shape[-2] * 4
    first = lax.axis_index("expert") * count
    lower = (
        lax.broadcasted_iota(jnp.int32, (rows, rows), 0)
        < lax.broadcasted_iota(jnp.int32, (rows, rows), 1)
    ).astype(jnp.bfloat16)
    slot = lax.broadcasted_iota(jnp.int32, (cap, rows), 0).astype(jnp.float32)
    picks = routes.shape[-2] // 2

    hits, gate_cols = [], []
    for b in range(blocks):
        rt = routes[0, b // 2, b % 2, :picks]
        gt = routes[0, b // 2, b % 2, picks:]
        hit_b, gate_b = [], []
        for j in range(count):
            hit = (rt == (first + j).astype(jnp.float32)).astype(jnp.float32)
            named = jnp.sum(hit, axis=0, keepdims=True)
            gate = jnp.sum(hit * gt, axis=0, keepdims=True)
            named8 = jnp.broadcast_to(named, (8, rows)).astype(jnp.bfloat16)
            rank = jnp.dot(named8, lower, preferred_element_type=jnp.float32)[:1]
            rank = jnp.where(named > 0.5, rank, -1.0)
            chosen = (slot == rank).astype(jnp.float32)
            gate_b.append(jnp.sum(chosen * gate, axis=1, keepdims=True))
            hit_b.append(hit)
            pick[b, j * cap:(j + 1) * cap] = chosen.astype(jnp.bfloat16)
        hits.append(hit_b)
        gate_cols.append(gate_b)

    for b in range(blocks):
        for src, dst in ((tok, x_rows), (cot, c_rows)):
            block = src[0, b // 2, b % 2].reshape(rows, width)
            got = jnp.dot(pick[b], block, preferred_element_type=jnp.float32)
            for j in range(count):
                dst[j, b * cap:(b + 1) * cap] = got[j * cap:(j + 1) * cap].astype(jnp.bfloat16)

    pairs = []
    for j in range(count):
        gate_pre = jnp.dot(x_rows[j], w_gate[j], preferred_element_type=jnp.float32)
        up_pre = jnp.dot(x_rows[j], w_up[j], preferred_element_type=jnp.float32)
        raw = jnp.dot(c_rows[j], w_down[j], preferred_element_type=jnp.float32)
        gate = jnp.concatenate([gate_cols[b][j] for b in range(blocks)], axis=0)
        sig = jax.nn.sigmoid(gate_pre)
        active = gate_pre * sig
        hidden = active * up_pre
        w_hidden[j] = (gate * hidden).astype(jnp.bfloat16)
        pairs.append(jnp.sum(raw * hidden, axis=1, keepdims=True))
        back = gate * raw
        d_gate[j] = (back * up_pre * sig * (1.0 + gate_pre * (1.0 - sig))).astype(jnp.bfloat16)
        d_up[j] = (back * active).astype(jnp.bfloat16)
        nt = (((1,), (1,)), ((), ()))
        out = lax.dot_general(w_hidden[j], w_down[j], nt, preferred_element_type=jnp.float32)
        row = lax.dot_general(d_gate[j], w_gate[j], nt, preferred_element_type=jnp.float32)
        row = row + lax.dot_general(d_up[j], w_up[j], nt, preferred_element_type=jnp.float32)
        for b in range(blocks):
            out_rows[b, j * cap:(j + 1) * cap] = out[b * cap:(b + 1) * cap].astype(jnp.bfloat16)
            row_rows[b, j * cap:(j + 1) * cap] = row[b * cap:(b + 1) * cap].astype(jnp.bfloat16)

    half = width // 2
    for b in range(blocks):
        total = jnp.zeros((picks, rows), jnp.float32)
        for j in range(count):
            chosen = pick[b, j * cap:(j + 1) * cap].astype(jnp.float32)
            line = jnp.sum(chosen * pairs[j][b * cap:(b + 1) * cap], axis=0, keepdims=True)
            total = total + hits[b][j] * line
        pair_part[0, b // 2, b % 2] = total
        tn = (((0,), (0,)), ((), ()))
        for src, dst in ((out_rows, out_part), (row_rows, row_part)):
            for f in range(2):
                dst[0, b // 2, b % 2, f] = lax.dot_general(
                    pick[b], src[b, :, f * half:(f + 1) * half], tn,
                    preferred_element_type=jnp.float32,
                ).astype(jnp.bfloat16)


def add_into(dst, *others):
    total = dst[...].astype(jnp.float32)
    for other in others:
        total = total + other[...].astype(jnp.float32)
    dst[...] = total.astype(dst.dtype)


R_CORE, R_X, R_Y, R_Y2, R_X2, R_Z, R_Z2 = range(7)


def collect_kernel(line, out_part, row_part, pair_part, mixed, token_grad, gates_grad,
                   held, held_pair, from_core, pair_core, from_x, from_y, from_y2, from_x2,
                   pair_x, pair_y, pair_sum, from_z, pair_z, send_sem, recv_sem, load_sem):
    p = Place(line)
    x, y, c, z = p.x, p.y, p.c, p.z
    rows = mixed.shape[0]
    cut = rows // 2
    parts = (out_part, row_part)
    order = (p.mate, p.inner, p.outer, z)
    loads = {}
    for s, far in enumerate(order):
        for t in range(2):
            loads[t, s] = pltpu.make_async_copy(
                parts[t].at[far, :, c], held.at[t, far], load_sem.at[t, s]
            )
            loads[t, s].start()
    load_pair = pltpu.make_async_copy(pair_part.at[:, :, c], held_pair, load_sem.at[2, 0])
    load_pair.start()
    greet(p)
    mail = Mail(send_sem, recv_sem)
    for s, far in enumerate(order):
        for t in range(2):
            mail.send(parts[t].at[far, :, 1 - c], from_core.at[t, far], (t, R_CORE, far), p.to_core)
    mail.send(pair_part.at[:, :, 1 - c], pair_core, (2, R_CORE, 0), p.to_core)

    for s, far in enumerate(order):
        for t in range(2):
            loads[t, s].wait()
            mail.wait(from_core.at[t, far], (t, R_CORE, far), p.to_core)
            add_into(held.at[t, far], from_core.at[t, far])
            mail.send(
                held.at[t, far, :, 1 - x, :cut], from_x.at[t, far], (t, R_X, far), p.to_x
            )
            mail.send(
                held.at[t, far, 1 - y, :, cut:], from_y.at[t, far], (t, R_Y, far), p.to_y
            )
    load_pair.wait()
    mail.wait(pair_core, (2, R_CORE, 0), p.to_core)
    add_into(held_pair, pair_core)
    mail.send(held_pair.at[:, 1 - y], pair_y, (2, R_Y, 0), p.to_y)

    for s, far in enumerate(order):
        for t in range(2):
            mail.wait(from_x.at[t, far], (t, R_X, far), p.to_x)
            add_into(held.at[t, far, :, x, :cut], from_x.at[t, far])
            mail.send(
                held.at[t, far, 1 - y, x, :cut], from_y2.at[t, far], (t, R_Y2, far), p.to_y
            )
            mail.wait(from_y.at[t, far], (t, R_Y, far), p.to_y)
            add_into(held.at[t, far, y, :, cut:], from_y.at[t, far])
            mail.send(
                held.at[t, far, y, 1 - x, cut:], from_x2.at[t, far], (t, R_X2, far), p.to_x
            )
    mail.wait(pair_y, (2, R_Y, 0), p.to_y)
    add_into(held_pair.at[:, y], pair_y)
    mail.send(held_pair.at[:, y], pair_x, (2, R_X, 0), p.to_x)

    def joined(t, far):
        mail.wait(from_y2.at[t, far], (t, R_Y2, far), p.to_y)
        add_into(held.at[t, far, y, x, :cut], from_y2.at[t, far])
        mail.wait(from_x2.at[t, far], (t, R_X2, far), p.to_x)
        add_into(held.at[t, far, y, x, cut:], from_x2.at[t, far])

    def pass_on(t, far, mine, arrived):
        rising = far > z

        @pl.when(rising & p.has_left)
        def _():
            mail.wait(arrived.at[far, 0], (t, R_Z, far), p.to_left)
            add_into(mine, arrived.at[far, 0])

        @pl.when(jnp.logical_not(rising) & p.has_right)
        def _():
            mail.wait(arrived.at[far, 1], (t, R_Z2, far), p.to_right)
            add_into(mine, arrived.at[far, 1])

        mail.send(mine, arrived.at[far, 0], (t, R_Z, far), p.to_right, when=rising)
        mail.send(
            mine, arrived.at[far, 1], (t, R_Z2, far), p.to_left, when=jnp.logical_not(rising)
        )

    def last(t, mine, arrived, dst):
        @pl.when(p.has_left)
        def _():
            mail.wait(arrived.at[z, 0], (t, R_Z, z), p.to_left)
            add_into(mine, arrived.at[z, 0])

        @pl.when(p.has_right)
        def _():
            mail.wait(arrived.at[z, 1], (t, R_Z2, z), p.to_right)
            add_into(mine, arrived.at[z, 1])

        dst[...] = mine[...]

    mail.wait(pair_x, (2, R_X, 0), p.to_x)
    pair_sum[...] = held_pair[:, y] + pair_x[...]
    for far in (p.inner, p.outer, p.mate):
        for t in range(2):
            joined(t, far)
            pass_on(t, far, held.at[t, far, y, x], from_z.at[t])
        pass_on(2, far, pair_sum.at[far], pair_z)
    for t, dst in ((0, mixed), (1, token_grad)):
        joined(t, z)
        last(t, held.at[t, z, y, x], from_z.at[t], dst)
    last(2, pair_sum.at[z], pair_z, gates_grad)
    mail.finish()


def body_lines(tokens, routing, route_gates, gate_weight, up_weight, down_weight, cotangent):
    rows, width = tokens.shape
    picks = routing.shape[1]
    count, _, hidden_units = gate_weight.shape
    devices = lax.axis_size("expert")
    line = devices // 4
    cap = 3 * rows * picks // (2 * count * devices)
    half = width // 2
    bf16, f32 = jnp.bfloat16, jnp.float32
    anywhere = pl.BlockSpec(memory_space=pl.ANY)
    in_vmem = pl.BlockSpec(memory_space=pltpu.VMEM)

    routes = jnp.concatenate([routing.astype(f32).T, route_gates.T], axis=0)
    quarters = (2, 2, rows // 4, width)
    all_tok, all_cot, all_routes = pl.pallas_call(
        functools.partial(spread_kernel, line),
        out_shape=[
            jax.ShapeDtypeStruct((line, 2, 2) + quarters, bf16),
            jax.ShapeDtypeStruct((line, 2, 2) + quarters, bf16),
            jax.ShapeDtypeStruct((line, 2, 2, 2 * picks, rows), f32),
        ],
        in_specs=[anywhere] * 3,
        out_specs=[anywhere] * 3,
        scratch_shapes=[
            pltpu.SemaphoreType.DMA((3, 7, line)),
            pltpu.SemaphoreType.DMA((3, 7, line)),
            pltpu.SemaphoreType.DMA((3,)),
        ],
        compiler_params=pltpu.CompilerParams(collective_id=0, has_side_effects=True),
        name="spread",
    )(tokens.reshape(quarters), cotangent.reshape(quarters), routes)

    slots = line * 4 * cap
    group = 4 * cap

    def stepped(shape, dim=0):
        def index(g):
            return tuple(g if i == dim else 0 for i in range(len(shape)))
        return pl.BlockSpec(shape, index)

    whole = pl.BlockSpec((count, width, hidden_units), lambda g: (0, 0, 0))
    out_part, row_part, pair_part, x_rows, c_rows, d_gate, d_up, w_hidden = pl.pallas_call(
        functools.partial(expert_kernel, cap),
        grid=(line,),
        out_shape=[
            jax.ShapeDtypeStruct((line, 2, 2, 2, rows, half), bf16),
            jax.ShapeDtypeStruct((line, 2, 2, 2, rows, half), bf16),
            jax.ShapeDtypeStruct((line, 2, 2, picks, rows), f32),
            jax.ShapeDtypeStruct((count, slots, width), bf16),
            jax.ShapeDtypeStruct((count, slots, width), bf16),
            jax.ShapeDtypeStruct((count, slots, hidden_units), bf16),
            jax.ShapeDtypeStruct((count, slots, hidden_units), bf16),
            jax.ShapeDtypeStruct((count, slots, hidden_units), bf16),
        ],
        in_specs=[
            stepped((1, 2, 2) + quarters),
            stepped((1, 2, 2) + quarters),
            stepped((1, 2, 2, 2 * picks, rows)),
            whole,
            whole,
            whole,
        ],
        out_specs=[
            stepped((1, 2, 2, 2, rows, half)),
            stepped((1, 2, 2, 2, rows, half)),
            stepped((1, 2, 2, picks, rows)),
            stepped((count, group, width), 1),
            stepped((count, group, width), 1),
            stepped((count, group, hidden_units), 1),
            stepped((count, group, hidden_units), 1),
            stepped((count, group, hidden_units), 1),
        ],
        scratch_shapes=[
            pltpu.VMEM((4, count * cap, rows), bf16),
            pltpu.VMEM((4, count * cap, width), bf16),
            pltpu.VMEM((4, count * cap, width), bf16),
        ],
        compiler_params=pltpu.CompilerParams(vmem_limit_bytes=58 << 20),
        name="experts",
    )(all_tok, all_cot, all_routes, gate_weight, up_weight, down_weight)

    cut = rows // 2
    mixed, token_grad, gates_grad = pl.pallas_call(
        functools.partial(collect_kernel, line),
        out_shape=[
            jax.ShapeDtypeStruct((rows, half), bf16),
            jax.ShapeDtypeStruct((rows, half), bf16),
            jax.ShapeDtypeStruct((picks, rows), f32),
        ],
        in_specs=[anywhere] * 3,
        out_specs=[in_vmem] * 3,
        scratch_shapes=[
            pltpu.VMEM((2, line, 2, 2, rows, half), bf16),
            pltpu.VMEM((line, 2, picks, rows), f32),
            pltpu.VMEM((2, line, 2, 2, rows, half), bf16),
            pltpu.VMEM((line, 2, picks, rows), f32),
            pltpu.VMEM((2, line, 2, cut, half), bf16),
            pltpu.VMEM((2, line, 2, cut, half), bf16),
            pltpu.VMEM((2, line, cut, half), bf16),
            pltpu.VMEM((2, line, cut, half), bf16),
            pltpu.VMEM((line, picks, rows), f32),
            pltpu.VMEM((line, picks, rows), f32),
            pltpu.VMEM((line, picks, rows), f32),
            pltpu.VMEM((2, line, 2, rows, half), bf16),
            pltpu.VMEM((line, 2, picks, rows), f32),
            pltpu.SemaphoreType.DMA((3, 7, line)),
            pltpu.SemaphoreType.DMA((3, 7, line)),
            pltpu.SemaphoreType.DMA((3, line)),
        ],
        compiler_params=pltpu.CompilerParams(
            collective_id=1, has_side_effects=True, vmem_limit_bytes=48 << 20
        ),
        name="collect",
    )(out_part, row_part, pair_part)

    def outer(a, b):
        return jnp.einsum("jrd,jrf->jdf", a, b, preferred_element_type=f32).astype(bf16)

    return (
        mixed,
        token_grad,
        gates_grad.T,
        outer(x_rows, d_gate),
        outer(x_rows, d_up),
        outer(c_rows, w_hidden),
    )


def body(tokens, *rest):
    devices = lax.axis_size("expert")
    if lax.axis_size("dp") == 2 and devices == 16:
        return body_lines(tokens, *rest)
    held = 8 * tokens.size * tokens.dtype.itemsize * devices
    return (body_whole if held < 1 << 27 else body_slots)(tokens, *rest)


def solution(mesh):
    in_specs = (
        P("expert", None),
        P("expert", None),
        P("expert", None),
        P("expert", None, "dp"),
        P("expert", None, "dp"),
        P("expert", None, "dp"),
        P("expert", None),
    )
    out_specs = (
        P("expert", "dp"),
        P("expert", "dp"),
        P("expert", None),
        P("expert", None, "dp"),
        P("expert", None, "dp"),
        P("expert", None, "dp"),
    )
    return jax.shard_map(body, mesh=mesh, in_specs=in_specs, out_specs=out_specs, check_vma=False)
```

```python
import functools
import types

import jax
import jax.numpy as jnp
from jax import lax
from jax.experimental import pallas as pl
from jax.experimental.pallas import tpu as pltpu
from jax.sharding import PartitionSpec as P


def dot(a, b, dims):
    return lax.dot_general(a, b, (dims, ((), ())), preferred_element_type=jnp.float32)


def body_whole(tokens, routing, route_gates, gate_weight, up_weight, down_weight, cotangent):
    local_count = gate_weight.shape[0]
    first = lax.axis_index("expert") * local_count

    all_tokens = lax.all_gather(tokens, "expert", axis=0, tiled=True)
    picks = routing.shape[1]
    routes = jnp.concatenate([routing.astype(jnp.float32), route_gates], axis=1)
    all_routes = lax.all_gather(routes, "expert", axis=0, tiled=True)
    all_routing, all_gates = all_routes[:, :picks].astype(jnp.int32), all_routes[:, picks:]
    all_cotangent = lax.all_gather(cotangent, "expert", axis=0, tiled=True)

    named = [all_routing == first + j for j in range(local_count)]
    gate_of = [
        jnp.sum(jnp.where(named[j], all_gates, 0.0), axis=1, keepdims=True)
        for j in range(local_count)
    ]

    saved = []
    mixed_part = None
    for j in range(local_count):
        gate_pre = dot(all_tokens, gate_weight[j], ((1,), (0,)))
        up_pre = dot(all_tokens, up_weight[j], ((1,), (0,)))
        sigmoid_gate = jax.nn.sigmoid(gate_pre)
        active = gate_pre * sigmoid_gate
        hidden = active * up_pre
        weighted_hidden = (gate_of[j] * hidden).astype(jnp.bfloat16)
        saved.append((gate_pre.astype(jnp.bfloat16), up_pre.astype(jnp.bfloat16), weighted_hidden))
    hidden_cat = jnp.concatenate([s[2] for s in saved], axis=1)
    down_cat = jnp.concatenate([down_weight[j] for j in range(local_count)], axis=1)
    mixed_part = dot(hidden_cat, down_cat, ((1,), (1,))).astype(jnp.bfloat16)
    mixed_rows = lax.psum_scatter(mixed_part, "expert", scatter_dimension=0, tiled=True)

    grads = []
    gates_part = 0.0
    for j in range(local_count):
        gate_pre, up_pre, weighted_hidden = saved[j]
        gate_pre, up_pre = gate_pre.astype(jnp.float32), up_pre.astype(jnp.float32)
        raw = dot(all_cotangent, down_weight[j], ((1,), (0,)))
        sigmoid_gate = jax.nn.sigmoid(gate_pre)
        active = gate_pre * sigmoid_gate
        pair = jnp.sum(raw * (active * up_pre), axis=1, keepdims=True)
        gates_part = gates_part + jnp.where(named[j], pair, 0.0)
        dhidden = gate_of[j] * raw
        d_gate = (dhidden * up_pre * sigmoid_gate * (1.0 + gate_pre * (1.0 - sigmoid_gate))).astype(
            jnp.bfloat16
        )
        d_up = (dhidden * active).astype(jnp.bfloat16)
        grads.append((d_gate, d_up))
    d_cat = jnp.concatenate([g for pair in grads for g in pair], axis=1)
    w_cat = jnp.concatenate(
        [w for j in range(local_count) for w in (gate_weight[j], up_weight[j])], axis=1
    )
    token_part = dot(d_cat, w_cat, ((1,), (1,))).astype(jnp.bfloat16)
    token_rows = lax.psum_scatter(token_part, "expert", scatter_dimension=0, tiled=True)
    mixed = lax.psum_scatter(mixed_rows, "dp", scatter_dimension=1, tiled=True)
    token_grad = lax.psum_scatter(token_rows, "dp", scatter_dimension=1, tiled=True)
    gates_grad = lax.psum(
        lax.psum_scatter(gates_part, "expert", scatter_dimension=0, tiled=True), "dp"
    )

    grad_g = jnp.stack([dot(all_tokens, g, ((0,), (0,))).astype(jnp.bfloat16) for g, _ in grads])
    grad_u = jnp.stack([dot(all_tokens, u, ((0,), (0,))).astype(jnp.bfloat16) for _, u in grads])
    grad_d = jnp.stack(
        [dot(all_cotangent, s[2], ((0,), (0,))).astype(jnp.bfloat16) for s in saved]
    )
    return (mixed, token_grad, gates_grad, grad_g, grad_u, grad_d)


def expert_forward(slot_rows, w_gate, w_up, w_down):
    gate_pre = jnp.einsum("jrd,jdf->jrf", slot_rows, w_gate, preferred_element_type=jnp.float32)
    up_pre = jnp.einsum("jrd,jdf->jrf", slot_rows, w_up, preferred_element_type=jnp.float32)
    sigmoid_gate = jax.nn.sigmoid(gate_pre)
    active = gate_pre * sigmoid_gate
    hidden = (active * up_pre).astype(jnp.bfloat16)
    out_part = jnp.einsum("jrf,jdf->jrd", hidden, w_down, preferred_element_type=jnp.float32)
    return (out_part, (gate_pre, up_pre, sigmoid_gate, active, hidden))


def expert_backward(slot_rows, slot_back, saved, w_gate, w_up, w_down):
    gate_pre, up_pre, sigmoid_gate, active, hidden = saved
    dhidden = jnp.einsum("jrd,jdf->jrf", slot_back, w_down, preferred_element_type=jnp.float32)
    d_gate = (dhidden * up_pre * sigmoid_gate * (1.0 + gate_pre * (1.0 - sigmoid_gate))).astype(
        jnp.bfloat16
    )
    d_up = (dhidden * active).astype(jnp.bfloat16)
    row_part = jnp.einsum("jrf,jdf->jrd", d_gate, w_gate, preferred_element_type=jnp.float32)
    row_part = row_part + jnp.einsum("jrf,jdf->jrd", d_up, w_up, preferred_element_type=jnp.float32)
    grad_g = jnp.einsum("jrd,jrf->jdf", slot_rows, d_gate, preferred_element_type=jnp.float32)
    grad_u = jnp.einsum("jrd,jrf->jdf", slot_rows, d_up, preferred_element_type=jnp.float32)
    grad_d = jnp.einsum("jrd,jrf->jdf", slot_back, hidden, preferred_element_type=jnp.float32)
    return (row_part, (grad_g, grad_u, grad_d))


def body_slots(tokens, routing, route_gates, gate_weight, up_weight, down_weight, cotangent):
    rows_here, width = tokens.shape
    picks = routing.shape[1]
    local_count = gate_weight.shape[0]
    devices = lax.axis_size("expert")
    experts_all = local_count * devices
    capacity = 3 * rows_here * picks // (2 * experts_all)
    member = lax.axis_index("dp")
    chosen = routing.reshape(-1)
    one_hot = (chosen[:, None] == jnp.arange(experts_all, dtype=jnp.int32)[None, :]).astype(
        jnp.int32
    )
    running = jnp.cumsum(one_hot, axis=0) - one_hot
    within = jnp.sum(running * one_hot, axis=1)
    owners = chosen // local_count
    slots = chosen % local_count
    source_row = jnp.arange(rows_here * picks, dtype=jnp.int32) // picks
    flat_gates = route_gates.reshape(-1)
    x_rows = tokens[source_row]
    weighted = (flat_gates[:, None] * cotangent[source_row].astype(jnp.float32)).astype(
        jnp.bfloat16
    )
    half_cap = (capacity + 1) // 2
    mine = within // half_cap == member
    local_within = jnp.clip(within - member * half_cap, 0, half_cap - 1)
    target = jnp.where(mine, owners, devices)

    def scatter_share(values):
        buffer = jnp.zeros((local_count, devices, half_cap) + values.shape[1:], values.dtype)
        return buffer.at[slots, target, local_within].set(values, mode="drop")

    def gather_share(buffer):
        picked = buffer.at[slots, target, local_within].get(mode="fill", fill_value=0)
        return jnp.where(mine[:, None], picked, jnp.zeros((), picked.dtype))

    full_gate, full_up, full_down = (
        lax.all_gather(gate_weight, "dp", axis=2, tiled=True),
        lax.all_gather(up_weight, "dp", axis=2, tiled=True),
        lax.all_gather(down_weight, "dp", axis=2, tiled=True),
    )
    got_rows, got_back = (
        lax.all_to_all(scatter_share(x_rows), "expert", split_axis=1, concat_axis=1, tiled=True),
        lax.all_to_all(scatter_share(weighted), "expert", split_axis=1, concat_axis=1, tiled=True),
    )
    slot_rows = got_rows.reshape(local_count, devices * half_cap, width)
    slot_back = got_back.reshape(local_count, devices * half_cap, width)
    out_full, saved = expert_forward(slot_rows, full_gate, full_up, full_down)
    row_full, grads_full = expert_backward(
        slot_rows, slot_back, saved, full_gate, full_up, full_down
    )
    share_shape = (local_count, devices, half_cap, width)
    back_out, back_grad = (
        lax.all_to_all(
            out_full.astype(jnp.bfloat16).reshape(share_shape),
            "expert",
            split_axis=1,
            concat_axis=1,
            tiled=True,
        ),
        lax.all_to_all(
            row_full.astype(jnp.bfloat16).reshape(share_shape),
            "expert",
            split_axis=1,
            concat_axis=1,
            tiled=True,
        ),
    )
    expert_rows = gather_share(back_out).reshape(rows_here, picks, width)
    grad_rows = gather_share(back_grad).reshape(rows_here, picks, width)
    gate_part = jnp.einsum("td,tkd->tk", cotangent, expert_rows, preferred_element_type=jnp.float32)
    mixed_part = jnp.einsum("tk,tkd->td", route_gates, expert_rows.astype(jnp.float32))
    token_part = jnp.sum(grad_rows.astype(jnp.float32), axis=1)
    mixed_sum, token_sum = (
        lax.psum_scatter(
            mixed_part.astype(jnp.bfloat16), "dp", scatter_dimension=1, tiled=True
        ).astype(jnp.float32),
        lax.psum_scatter(
            token_part.astype(jnp.bfloat16), "dp", scatter_dimension=1, tiled=True
        ).astype(jnp.float32),
    )
    mixed = mixed_sum.astype(jnp.bfloat16)
    token_grad = token_sum.astype(jnp.bfloat16)
    grad_g, grad_u, grad_d = (
        lax.psum_scatter(
            grads_full[0].astype(jnp.bfloat16), "dp", scatter_dimension=2, tiled=True
        ).astype(jnp.float32),
        lax.psum_scatter(
            grads_full[1].astype(jnp.bfloat16), "dp", scatter_dimension=2, tiled=True
        ).astype(jnp.float32),
        lax.psum_scatter(
            grads_full[2].astype(jnp.bfloat16), "dp", scatter_dimension=2, tiled=True
        ).astype(jnp.float32),
    )
    grad_g = grad_g.astype(jnp.bfloat16)
    grad_u = grad_u.astype(jnp.bfloat16)
    grad_d = grad_d.astype(jnp.bfloat16)
    gates_grad = lax.psum(gate_part, "dp")
    return (mixed, token_grad, gates_grad, grad_g, grad_u, grad_d)


MESH = pl.DeviceIdType.MESH


class Place:
    def __init__(self, line):
        self.x = lax.axis_index("dp")
        self.e = lax.axis_index("expert")
        self.line = line
        self.z = self.e // 4
        self.y = (self.e // 2) % 2
        self.c = self.e % 2
        self.to_x = (1 - self.x, self.e)
        self.to_y = (self.x, self.e + 2 - 4 * self.y)
        self.to_core = (self.x, self.e + 1 - 2 * self.c)
        half = self.z // 2
        self.mate = self.z + 1 - 2 * (self.z % 2)
        self.inner = 2 - half
        self.outer = 3 - 3 * half
        self.between = (self.z > 0) & (self.z < line - 1)
        self.at_end = jnp.logical_not(self.between)
        self.others = (self.mate, self.inner, self.outer)

    def along(self, far):
        return (self.x, far * 4 + self.y * 2 + self.c)

    def group(self, s):
        low, high = s % 2, s // 2
        near = self.z * (1 - low) + self.mate * low
        rest = self.inner * (1 - low) + self.outer * low
        return near * (1 - high) + rest * high


def greet(p):
    barrier = pltpu.get_barrier_semaphore()
    peers = (p.to_x, p.to_y, p.to_core) + tuple(p.along(far) for far in p.others)
    for to in peers:
        pl.semaphore_signal(barrier, inc=1, device_id=to, device_id_type=MESH)
    pl.semaphore_wait(barrier, len(peers))


class Mail:
    def __init__(self, send_sem, recv_sem):
        self.send_sem, self.recv_sem, self.closing = send_sem, recv_sem, False

    def copy(self, src, dst, slot, to, send_slot=None):
        return pltpu.make_async_remote_copy(
            src_ref=src,
            dst_ref=dst,
            send_sem=self.send_sem.at[send_slot or slot],
            recv_sem=self.recv_sem.at[slot],
            device_id=to,
            device_id_type=MESH,
        )

    def send(self, src, dst, slot, to, send_slot=None):
        copy = self.copy(src, dst, slot, to, send_slot)
        if self.closing:
            copy.wait_send()
        else:
            copy.start()

    def wait(self, dst, slot, to):
        if not self.closing:
            self.copy(dst, dst, slot, to).wait_recv()

    def add(self, dst, *others):
        if not self.closing:
            total = dst[...].astype(jnp.float32)
            for other in others:
                total = total + other[...].astype(jnp.float32)
            dst[...] = total.astype(dst.dtype)


Z_IN, Y_ONE, X_TWO, X_ONE, Y_TWO, CORE, Z_OUT = range(7)
R_CORE, R_X, R_Y, R_Y2, R_X2, R_Z, R_Z_OUT = range(7, 14)
KINDS = 14


class Spread:
    def __init__(self, p, mail, pairs, routes, all_routes, own_sem):
        self.p, self.mail, self.pairs = p, mail, pairs
        self.routes, self.all_routes, self.own_sem = routes, all_routes, own_sem

    def own_copies(self):
        p = self.p
        found = self.pairs + ((self.routes, self.all_routes),)
        return [
            pltpu.make_async_copy(src, dst.at[p.z, p.y, p.c], self.own_sem.at[t])
            for t, (src, dst) in enumerate(found)
        ]

    def own_one(self):
        p, mail = self.p, self.mail
        for t, (src, dst) in enumerate(self.pairs):
            mail.send(src.at[p.x], dst.at[p.z, p.y, p.c, p.x], (t, Y_ONE, p.z), p.to_y)

    def own_to(self, far):
        p, mail = self.p, self.mail
        for t, (src, dst) in enumerate(self.pairs):
            piece = dst.at[p.z, p.y, p.c, p.x]
            mail.send(src.at[p.x], piece, (t, Z_IN, p.z), p.along(far), (t, Z_OUT, far))

    def routes_z(self):
        p, mail = self.p, self.mail
        here = self.all_routes.at[p.z, p.y, p.c]
        for far in p.others:
            mail.send(self.routes, here, (2, Z_IN, p.z), p.along(far), (2, Z_OUT, far))

    def own_two(self):
        p, mail = self.p, self.mail
        for t, (_, dst) in enumerate(self.pairs):
            piece = dst.at[p.z, 1 - p.y, p.c, p.x]
            mail.wait(piece, (t, Y_ONE, p.z), p.to_y)
            mail.send(piece, piece, (t, X_TWO, p.z), p.to_x)

    def own_three(self):
        p, mail = self.p, self.mail
        for t, (_, dst) in enumerate(self.pairs):
            mail.wait(dst.at[p.z, 1 - p.y, p.c, 1 - p.x], (t, X_TWO, p.z), p.to_x)
            mail.send(dst.at[p.z, :, p.c], dst.at[p.z, :, p.c], (t, CORE, p.z), p.to_core)

    def routes_y(self):
        p, mail, al = self.p, self.mail, self.all_routes
        for far in p.others:
            mail.wait(al.at[far, p.y, p.c], (2, Z_IN, far), p.along(far))
        mail.send(al.at[:, p.y, p.c], al.at[:, p.y, p.c], (2, Y_ONE, 0), p.to_y)

    def routes_core(self):
        p, mail, al = self.p, self.mail, self.all_routes
        mail.wait(al.at[:, 1 - p.y, p.c], (2, Y_ONE, 0), p.to_y)
        mail.send(al.at[:, :, p.c], al.at[:, :, p.c], (2, CORE, 0), p.to_core)

    def routes_end(self):
        p = self.p
        self.mail.wait(self.all_routes.at[:, :, 1 - p.c], (2, CORE, 0), p.to_core)

    def arrive(self, far, onward):
        p, mail = self.p, self.mail
        for t, (_, dst) in enumerate(self.pairs):
            piece = dst.at[far, p.y, p.c, p.x]
            mail.wait(piece, (t, Z_IN, far), p.along(far))
            if onward:
                mail.send(piece, piece, (t, Z_IN, far), p.along(p.mate))

    def one(self, t, far):
        p, mail = self.p, self.mail
        piece = self.pairs[t][1].at[far, p.y, p.c, p.x]
        mail.send(piece.at[0], piece.at[0], (t, Y_ONE, far), p.to_y)
        mail.send(piece.at[1], piece.at[1], (t, X_ONE, far), p.to_x)

    def two(self, t, far):
        p, mail = self.p, self.mail
        dst = self.pairs[t][1]
        mail.wait(dst.at[far, 1 - p.y, p.c, p.x, 0], (t, Y_ONE, far), p.to_y)
        both = dst.at[far, :, p.c, p.x, 0]
        mail.send(both, both, (t, X_TWO, far), p.to_x)
        mail.wait(dst.at[far, p.y, p.c, 1 - p.x, 1], (t, X_ONE, far), p.to_x)
        both = dst.at[far, p.y, p.c, :, 1]
        mail.send(both, both, (t, Y_TWO, far), p.to_y)

    def three(self, far):
        p, mail = self.p, self.mail
        for t, (_, dst) in enumerate(self.pairs):
            mail.wait(dst.at[far, :, p.c, 1 - p.x, 0], (t, X_TWO, far), p.to_x)
            mail.wait(dst.at[far, 1 - p.y, p.c, :, 1], (t, Y_TWO, far), p.to_y)
            mail.send(dst.at[far, :, p.c], dst.at[far, :, p.c], (t, CORE, far), p.to_core)

    def end(self, far):
        p = self.p
        for t, (_, dst) in enumerate(self.pairs):
            self.mail.wait(dst.at[far, :, 1 - p.c], (t, CORE, far), p.to_core)


class Collect:
    def __init__(self, p, mail, refs):
        vars(self).update(vars(refs))
        self.p, self.mail = p, mail
        self.cut = self.held.shape[-2] // 2

    def one(self, s, far):
        p, mail = self.p, self.mail

        @pl.when(s >= 2)
        def _():
            pl.semaphore_wait(self.free_sem, 1)

        for t in range(2):
            mail.send(self.stage.at[t], self.from_core.at[t, s % 2], (t, R_CORE, far), p.to_core)

    def merge(self, s, far):
        p, mail = self.p, self.mail
        for t in range(2):
            slot = self.from_core.at[t, s % 2]
            mail.copy(self.stage.at[t], slot, (t, R_CORE, far), p.to_core).wait()
            mail.add(self.held.at[t, far], slot)

        @pl.when(s < p.line - 2)
        def _():
            pl.semaphore_signal(
                self.free_sem, inc=1, device_id=p.to_core, device_id_type=MESH
            )

    def two(self, far):
        p, mail, held, cut = self.p, self.mail, self.held, self.cut
        for t in range(2):
            mail.send(
                held.at[t, far, :, 1 - p.x, :cut], self.from_x.at[t, far], (t, R_X, far), p.to_x
            )
            mail.send(
                held.at[t, far, 1 - p.y, :, cut:], self.from_y.at[t, far], (t, R_Y, far), p.to_y
            )

    def three(self, far):
        p, mail, held, cut = self.p, self.mail, self.held, self.cut
        for t in range(2):
            mail.wait(self.from_x.at[t, far], (t, R_X, far), p.to_x)
            mail.add(held.at[t, far, :, p.x, :cut], self.from_x.at[t, far])
            mail.send(
                held.at[t, far, 1 - p.y, p.x, :cut], self.from_y2.at[t, far], (t, R_Y2, far), p.to_y
            )
            mail.wait(self.from_y.at[t, far], (t, R_Y, far), p.to_y)
            mail.add(held.at[t, far, p.y, :, cut:], self.from_y.at[t, far])
            mail.send(
                held.at[t, far, p.y, 1 - p.x, cut:], self.from_x2.at[t, far], (t, R_X2, far), p.to_x
            )

    def joined(self, t, far):
        p, mail, held, cut = self.p, self.mail, self.held, self.cut
        mail.wait(self.from_y2.at[t, far], (t, R_Y2, far), p.to_y)
        mail.add(held.at[t, far, p.y, p.x, :cut], self.from_y2.at[t, far])
        mail.wait(self.from_x2.at[t, far], (t, R_X2, far), p.to_x)
        mail.add(held.at[t, far, p.y, p.x, cut:], self.from_x2.at[t, far])

    def pass_on(self, t, far, mine, arrived):
        p = self.p
        self.mail.send(mine, arrived.at[p.z], (t, R_Z, p.z), p.along(far), (t, R_Z_OUT, far))

    def last(self, t, mine, arrived, dst):
        p, mail = self.p, self.mail
        total = mine[...].astype(jnp.float32)
        for far in p.others:
            mail.wait(arrived.at[far], (t, R_Z, far), p.along(far))
            total = total + arrived[far].astype(jnp.float32)
        dst[...] = total.astype(dst.dtype)

    def four(self, far):
        p = self.p
        for t in range(2):
            self.joined(t, far)
            self.pass_on(t, far, self.held.at[t, far, p.y, p.x], self.from_z.at[t])

    def pair_on(self, far):
        self.pass_on(2, far, self.pair_sum.at[far], self.pair_z)

    def four_own(self, mixed, token_grad, gates_grad):
        p = self.p
        for t, dst in ((0, mixed), (1, token_grad)):
            self.joined(t, p.z)
            self.last(t, self.held.at[t, p.z, p.y, p.x], self.from_z.at[t], dst)
        self.last(2, self.pair_sum.at[p.z], self.pair_z, gates_grad)

    def pair_one(self):
        self.mail.send(self.pair_stage, self.pair_core, (2, R_CORE, 0), self.p.to_core)

    def pair_two(self):
        p, mail = self.p, self.mail
        mail.wait(self.pair_core, (2, R_CORE, 0), p.to_core)
        mail.add(self.held_pair, self.pair_core)
        mail.send(self.held_pair.at[:, 1 - p.y], self.pair_y, (2, R_Y, 0), p.to_y)

    def pair_three(self):
        p, mail = self.p, self.mail
        mail.wait(self.pair_y, (2, R_Y, 0), p.to_y)
        mail.add(self.held_pair.at[:, p.y], self.pair_y)
        mail.send(self.held_pair.at[:, p.y], self.pair_x, (2, R_X, 0), p.to_x)

    def pair_four(self):
        p = self.p
        self.mail.wait(self.pair_x, (2, R_X, 0), p.to_x)
        self.pair_sum[...] = self.held_pair[:, p.y] + self.pair_x[...]


def experts(cap, p, s, far, tok, cot, routes, w_gate, w_up, w_down, held, stage, held_pair,
            pair_stage, x_rows, c_rows, d_both, w_hidden, pick):
    count, width, hidden_units = w_gate.shape
    blocks = 4
    group = blocks * cap
    rows = routes.shape[-1]
    picks = routes.shape[-2] // 2
    first = p.e * count
    start = pl.multiple_of(s * group, group)
    lower = (
        lax.broadcasted_iota(jnp.int32, (rows, rows), 0)
        < lax.broadcasted_iota(jnp.int32, (rows, rows), 1)
    ).astype(jnp.bfloat16)
    slot = lax.broadcasted_iota(jnp.int32, (cap, rows), 0).astype(jnp.float32)
    place = [(b // 2, (p.c + b % 2) % 2) for b in range(blocks)]

    hits, gate_cols = [], []
    for b, (yy, cc) in enumerate(place):
        rt = routes[far, yy, cc, :picks]
        gt = routes[far, yy, cc, picks:]
        hit_b, gate_b = [], []
        for j in range(count):
            hit = (rt == (first + j).astype(jnp.float32)).astype(jnp.float32)
            named = jnp.sum(hit, axis=0, keepdims=True)
            gate = jnp.sum(hit * gt, axis=0, keepdims=True)
            named8 = jnp.broadcast_to(named, (8, rows)).astype(jnp.bfloat16)
            rank = jnp.dot(named8, lower, preferred_element_type=jnp.float32)[:1]
            rank = jnp.where(named > 0.5, rank, -1.0)
            chosen = (slot == rank).astype(jnp.float32)
            gate_b.append(jnp.sum(chosen * gate, axis=1, keepdims=True))
            hit_b.append(hit)
            pick[b, j * cap:(j + 1) * cap] = chosen.astype(jnp.bfloat16)
        hits.append(hit_b)
        gate_cols.append(gate_b)

    for b, (yy, cc) in enumerate(place):
        for src, dst in ((tok, x_rows), (cot, c_rows)):
            block = src[yy, cc].reshape(rows, width)
            got = jnp.dot(pick[b], block, preferred_element_type=jnp.float32)
            for j in range(count):
                at = pl.ds(pl.multiple_of(start + b * cap, 16), cap)
                dst[j, at] = got[j * cap:(j + 1) * cap].astype(jnp.bfloat16)

    at = pl.ds(start, group)
    pairs = []
    for j in range(count):
        gate_pre = jnp.dot(x_rows[j, at], w_gate[j], preferred_element_type=jnp.float32)
        up_pre = jnp.dot(x_rows[j, at], w_up[j], preferred_element_type=jnp.float32)
        raw = jnp.dot(c_rows[j, at], w_down[j], preferred_element_type=jnp.float32)
        gate = jnp.concatenate([gate_cols[b][j] for b in range(blocks)], axis=0)
        sig = jax.nn.sigmoid(gate_pre)
        active = gate_pre * sig
        hidden = active * up_pre
        back = gate * raw
        wh = (gate * hidden).astype(jnp.bfloat16)
        dg = (back * up_pre * sig * (1.0 + gate_pre * (1.0 - sig))).astype(jnp.bfloat16)
        du = (back * active).astype(jnp.bfloat16)
        w_hidden[j, at] = wh
        d_both[j, at, :hidden_units] = dg
        d_both[j, at, hidden_units:] = du
        pairs.append(jnp.sum(raw * hidden, axis=1, keepdims=True))
        nt = (((1,), (1,)), ((), ()))
        out = lax.dot_general(wh, w_down[j], nt, preferred_element_type=jnp.float32)
        row = lax.dot_general(dg, w_gate[j], nt, preferred_element_type=jnp.float32)
        row = row + lax.dot_general(du, w_up[j], nt, preferred_element_type=jnp.float32)
        for b, (yy, cc) in enumerate(place):
            for q in range(0, cap, 16):
                piece, low = divmod(j * cap + q, tok.shape[-2])
                to = (yy, cc, piece // 2, piece % 2, slice(low, low + 16))
                tok[to] = out[b * cap + q:b * cap + q + 16].astype(jnp.bfloat16)
                cot[to] = row[b * cap + q:b * cap + q + 16].astype(jnp.bfloat16)

    half = width // 2
    for b, (yy, cc) in enumerate(place):
        total = jnp.zeros((picks, rows), jnp.float32)
        for j in range(count):
            chosen = pick[b, j * cap:(j + 1) * cap].astype(jnp.float32)
            line = jnp.sum(chosen * pairs[j][b * cap:(b + 1) * cap], axis=0, keepdims=True)
            total = total + hits[b][j] * line
        if b % 2 == 0:
            held_pair[far, yy] = total
        else:
            pair_stage[far, yy] = total
        tn = (((0,), (0,)), ((), ()))
        for t, src in enumerate((tok, cot)):
            found = src[yy, cc].reshape(rows, width)
            for f in range(2):
                value = lax.dot_general(
                    pick[b], found[:count * cap, f * half:(f + 1) * half], tn,
                    preferred_element_type=jnp.float32,
                ).astype(jnp.bfloat16)
                if b % 2 == 0:
                    held[t, far, yy, f] = value
                else:
                    stage[t, yy, f] = value


def weight_grads(j, m, rows, d_rows, *grads):
    width, hidden_units = grads[0].shape[-2:]
    chunk = width // 8

    def part(k, carry):
        at = pl.ds(pl.multiple_of(k * chunk, chunk), chunk)
        value = lax.dot_general(
            rows[j, :, at], d_rows[j], (((0,), (0,)), ((), ())),
            preferred_element_type=jnp.float32,
        ).astype(jnp.bfloat16)
        for i, grad in enumerate(grads):
            grad[j, at] = value[:, i * hidden_units:(i + 1) * hidden_units]
        return carry

    lax.fori_loop(2 * m, 2 * m + 2, part, 0)


def layer_kernel(line, cap, names, *refs):
    r = types.SimpleNamespace(**dict(zip(names, refs)))
    p = Place(line)
    mail = Mail(r.send_sem, r.recv_sem)
    pairs = ((r.tok, r.all_tok), (r.cot, r.all_cot))
    spread = Spread(p, mail, pairs, r.routes, r.all_routes, r.own_sem)
    collect = Collect(p, mail, r)
    own = spread.own_copies()
    for copy in own:
        copy.start()
    weights = [
        pltpu.make_async_copy(src, dst, r.load_sem.at[i])
        for i, (src, dst) in enumerate(
            ((r.w_gate, r.w_gate_in), (r.w_up, r.w_up_in), (r.w_down, r.w_down_in))
        )
    ]
    greet(p)
    spread.own_one()
    spread.own_to(p.mate)
    spread.routes_z()
    spread.own_to(p.inner)
    for copy in weights:
        copy.start()

    def first_phase():
        spread.own_two()
        spread.arrive(p.mate, False)
        for t in range(2):
            spread.one(t, p.mate)
        spread.two(0, p.mate)
        if not mail.closing:
            for copy in own:
                copy.wait()
        spread.own_three()
        pl.when(p.between)(functools.partial(spread.arrive, p.inner, True))
        spread.routes_y()
        spread.two(1, p.mate)
        spread.routes_core()

    def second_phase():
        pl.when(p.at_end)(functools.partial(spread.arrive, p.inner, False))
        for t in range(2):
            spread.one(t, p.inner)
        pl.when(p.between)(functools.partial(spread.arrive, p.outer, True))
        spread.three(p.mate)
        for t in range(2):
            spread.two(t, p.inner)

    def third_phase():
        pl.when(p.at_end)(functools.partial(spread.arrive, p.outer, False))
        for t in range(2):
            spread.one(t, p.outer)
        spread.three(p.inner)
        for t in range(2):
            spread.two(t, p.outer)

    def fourth_phase():
        spread.three(p.outer)
        collect.two(p.mate)

    first_phase()
    for copy in weights:
        copy.wait()
    spread.routes_end()

    def grads_of(j, m):
        at = pl.ds(m * (r.w_gate.shape[1] // 4), r.w_gate.shape[1] // 4)
        return [
            pltpu.make_async_copy(src.at[j, at], dst.at[j, at], r.save_sem.at[i, j, m])
            for i, (src, dst) in enumerate(
                ((r.w_gate_in, r.gate_grad), (r.w_up_in, r.up_grad), (r.w_down_in, r.down_grad))
            )
        ]

    def gate_up_grads(j, m):
        weight_grads(j, m, r.x_rows, r.d_both, r.w_gate_in, r.w_up_in)
        for copy in grads_of(j, m)[:2]:
            copy.start()

    def down_grads(j, m):
        weight_grads(j, m, r.c_rows, r.w_hidden, r.w_down_in)
        grads_of(j, m)[2].start()

    def step(s, carry):
        far = p.group(s)
        pl.when(s == 1)(second_phase)
        pl.when(s == 2)(third_phase)
        pl.when(s == 3)(fourth_phase)
        spread.end(far)
        loads = [
            pltpu.make_async_copy(src.at[far], dst, r.load_sem.at[i])
            for i, (src, dst) in enumerate(((r.all_tok, r.tok_in), (r.all_cot, r.cot_in)))
        ]
        for copy in loads:
            copy.start()

        @pl.when(s > 0)
        def _():
            collect.merge(s - 1, p.group(s - 1))

        @pl.when(s == 3)
        def _():
            collect.two(p.inner)

        for copy in loads:
            copy.wait()
        experts(
            cap, p, s, far, r.tok_in, r.cot_in, r.all_routes, r.w_gate_in,
            r.w_up_in, r.w_down_in, r.held, r.stage, r.held_pair, r.pair_stage,
            r.x_rows, r.c_rows, r.d_both, r.w_hidden, r.pick,
        )
        collect.one(s, far)
        return carry

    lax.fori_loop(0, line, step, 0)
    count = r.w_gate.shape[0]
    work = [
        functools.partial(f, j, m)
        for j in range(count) for m in range(4) for f in (gate_up_grads, down_grads)
    ]

    whole = len(work)

    def some_work(parts):
        for piece in work[:parts * whole // 16]:
            piece()
        del work[:parts * whole // 16]

    collect.pair_one()
    collect.merge(line - 1, p.outer)
    collect.two(p.outer)
    collect.three(p.inner)
    collect.three(p.mate)
    collect.two(p.z)
    collect.pair_two()
    some_work(4)
    collect.four(p.inner)
    collect.four(p.mate)
    collect.three(p.outer)
    collect.pair_three()
    collect.four(p.outer)
    some_work(2)
    collect.three(p.z)
    collect.pair_four()
    for far in p.others:
        collect.pair_on(far)
    some_work(16)
    collect.four_own(r.mixed, r.token_grad, r.gates_grad)
    for j in range(count):
        for m in range(4):
            for copy in grads_of(j, m):
                copy.wait()

    mail.closing = True
    spread.own_one()
    spread.own_to(p.mate)
    spread.routes_z()
    spread.own_to(p.inner)
    first_phase()
    second_phase()
    third_phase()
    fourth_phase()
    collect.pair_one()
    for far in (p.inner, p.outer, p.z,):
        collect.two(far)
    for far in (p.mate, p.inner, p.outer, p.z,):
        collect.three(far)
    collect.pair_two()
    collect.pair_three()
    for far in p.others:
        for t in range(2):
            collect.pass_on(t, far, r.held.at[t, far, p.y, p.x], r.from_z.at[t])
        collect.pair_on(far)


def body_lines(tokens, routing, route_gates, gate_weight, up_weight, down_weight, cotangent):
    rows, width = tokens.shape
    picks = routing.shape[1]
    count, _, hidden_units = gate_weight.shape
    devices = lax.axis_size("expert")
    line = devices // 4
    cap = 3 * rows * picks // (2 * count * devices)
    half, cut = width // 2, rows // 2
    slots = line * 4 * cap
    bf16, f32 = jnp.bfloat16, jnp.float32
    anywhere = pl.BlockSpec(memory_space=pl.ANY)
    in_vmem = pl.BlockSpec(memory_space=pltpu.VMEM)

    routes = jnp.concatenate([routing.astype(f32).T, route_gates.T], axis=0)
    quarters = (2, 2, rows // 4, width)
    inputs = dict(
        tok=tokens.reshape(quarters),
        cot=cotangent.reshape(quarters),
        routes=routes,
        w_gate=gate_weight,
        w_up=up_weight,
        w_down=down_weight,
    )
    shape = jax.ShapeDtypeStruct
    outs = dict(
        mixed=(shape((rows, half), bf16), in_vmem),
        token_grad=(shape((rows, half), bf16), in_vmem),
        gates_grad=(shape((picks, rows), f32), in_vmem),
        gate_grad=(shape(gate_weight.shape, bf16), anywhere),
        up_grad=(shape(gate_weight.shape, bf16), anywhere),
        down_grad=(shape(gate_weight.shape, bf16), anywhere),
        all_tok=(shape((line, 2, 2) + quarters, bf16), anywhere),
        all_cot=(shape((line, 2, 2) + quarters, bf16), anywhere),
    )
    weight = pltpu.VMEM((count, width, hidden_units), bf16)
    scratch = dict(
        all_routes=pltpu.VMEM((line, 2, 2, 2 * picks, rows), f32),
        w_gate_in=weight,
        w_up_in=weight,
        w_down_in=weight,
        tok_in=pltpu.VMEM((2, 2) + quarters, bf16),
        cot_in=pltpu.VMEM((2, 2) + quarters, bf16),
        x_rows=pltpu.VMEM((count, slots, width), bf16),
        c_rows=pltpu.VMEM((count, slots, width), bf16),
        d_both=pltpu.VMEM((count, slots, 2 * hidden_units), bf16),
        w_hidden=pltpu.VMEM((count, slots, hidden_units), bf16),
        pick=pltpu.VMEM((4, count * cap, rows), bf16),
        held=pltpu.VMEM((2, line, 2, 2, rows, half), bf16),
        stage=pltpu.VMEM((2, 2, 2, rows, half), bf16),
        from_core=pltpu.VMEM((2, 2, 2, 2, rows, half), bf16),
        from_x=pltpu.VMEM((2, line, 2, cut, half), bf16),
        from_y=pltpu.VMEM((2, line, 2, cut, half), bf16),
        from_y2=pltpu.VMEM((2, line, cut, half), bf16),
        from_x2=pltpu.VMEM((2, line, cut, half), bf16),
        from_z=pltpu.VMEM((2, line, rows, half), bf16),
        held_pair=pltpu.VMEM((line, 2, picks, rows), f32),
        pair_stage=pltpu.VMEM((line, 2, picks, rows), f32),
        pair_core=pltpu.VMEM((line, 2, picks, rows), f32),
        pair_y=pltpu.VMEM((line, picks, rows), f32),
        pair_x=pltpu.VMEM((line, picks, rows), f32),
        pair_sum=pltpu.VMEM((line, picks, rows), f32),
        pair_z=pltpu.VMEM((line, picks, rows), f32),
        send_sem=pltpu.SemaphoreType.DMA((3, KINDS, line)),
        recv_sem=pltpu.SemaphoreType.DMA((3, KINDS, line)),
        free_sem=pltpu.SemaphoreType.REGULAR,
        own_sem=pltpu.SemaphoreType.DMA((3,)),
        load_sem=pltpu.SemaphoreType.DMA((3,)),
        save_sem=pltpu.SemaphoreType.DMA((3, count, 4)),
    )
    names = list(inputs) + list(outs) + list(scratch)
    got = pl.pallas_call(
        functools.partial(layer_kernel, line, cap, names),
        out_shape=[v[0] for v in outs.values()],
        in_specs=[anywhere] * len(inputs),
        out_specs=[v[1] for v in outs.values()],
        scratch_shapes=list(scratch.values()),
        compiler_params=pltpu.CompilerParams(
            collective_id=0, has_side_effects=True, vmem_limit_bytes=64 << 20
        ),
        name="layer",
    )(*inputs.values())
    got = types.SimpleNamespace(**dict(zip(outs, got)))

    return (
        got.mixed,
        got.token_grad,
        got.gates_grad.T,
        got.gate_grad,
        got.up_grad,
        got.down_grad,
    )


def body(tokens, *rest):
    devices = lax.axis_size("expert")
    if lax.axis_size("dp") == 2 and devices == 16:
        return body_lines(tokens, *rest)
    held = 8 * tokens.size * tokens.dtype.itemsize * devices
    return (body_whole if held < 1 << 27 else body_slots)(tokens, *rest)


def solution(mesh):
    in_specs = (
        P("expert", None),
        P("expert", None),
        P("expert", None),
        P("expert", None, "dp"),
        P("expert", None, "dp"),
        P("expert", None, "dp"),
        P("expert", None),
    )
    out_specs = (
        P("expert", "dp"),
        P("expert", "dp"),
        P("expert", None),
        P("expert", None, "dp"),
        P("expert", None, "dp"),
        P("expert", None, "dp"),
    )
    return jax.shard_map(body, mesh=mesh, in_specs=in_specs, out_specs=out_specs, check_vma=False)
```

```python
import functools
import types

import jax
import jax.numpy as jnp
from jax import lax
from jax.experimental import pallas as pl
from jax.experimental.pallas import tpu as pltpu
from jax.sharding import PartitionSpec as P


def dot(a, b, dims):
    return lax.dot_general(a, b, (dims, ((), ())), preferred_element_type=jnp.float32)


def body_whole(tokens, routing, route_gates, gate_weight, up_weight, down_weight, cotangent):
    local_count = gate_weight.shape[0]
    first = lax.axis_index("expert") * local_count

    all_tokens = lax.all_gather(tokens, "expert", axis=0, tiled=True)
    picks = routing.shape[1]
    routes = jnp.concatenate([routing.astype(jnp.float32), route_gates], axis=1)
    all_routes = lax.all_gather(routes, "expert", axis=0, tiled=True)
    all_routing, all_gates = all_routes[:, :picks].astype(jnp.int32), all_routes[:, picks:]
    all_cotangent = lax.all_gather(cotangent, "expert", axis=0, tiled=True)

    named = [all_routing == first + j for j in range(local_count)]
    gate_of = [
        jnp.sum(jnp.where(named[j], all_gates, 0.0), axis=1, keepdims=True)
        for j in range(local_count)
    ]

    saved = []
    mixed_part = None
    for j in range(local_count):
        gate_pre = dot(all_tokens, gate_weight[j], ((1,), (0,)))
        up_pre = dot(all_tokens, up_weight[j], ((1,), (0,)))
        sigmoid_gate = jax.nn.sigmoid(gate_pre)
        active = gate_pre * sigmoid_gate
        hidden = active * up_pre
        weighted_hidden = (gate_of[j] * hidden).astype(jnp.bfloat16)
        saved.append((gate_pre.astype(jnp.bfloat16), up_pre.astype(jnp.bfloat16), weighted_hidden))
    hidden_cat = jnp.concatenate([s[2] for s in saved], axis=1)
    down_cat = jnp.concatenate([down_weight[j] for j in range(local_count)], axis=1)
    mixed_part = dot(hidden_cat, down_cat, ((1,), (1,))).astype(jnp.bfloat16)
    mixed_rows = lax.psum_scatter(mixed_part, "expert", scatter_dimension=0, tiled=True)

    grads = []
    gates_part = 0.0
    for j in range(local_count):
        gate_pre, up_pre, weighted_hidden = saved[j]
        gate_pre, up_pre = gate_pre.astype(jnp.float32), up_pre.astype(jnp.float32)
        raw = dot(all_cotangent, down_weight[j], ((1,), (0,)))
        sigmoid_gate = jax.nn.sigmoid(gate_pre)
        active = gate_pre * sigmoid_gate
        pair = jnp.sum(raw * (active * up_pre), axis=1, keepdims=True)
        gates_part = gates_part + jnp.where(named[j], pair, 0.0)
        dhidden = gate_of[j] * raw
        d_gate = (dhidden * up_pre * sigmoid_gate * (1.0 + gate_pre * (1.0 - sigmoid_gate))).astype(
            jnp.bfloat16
        )
        d_up = (dhidden * active).astype(jnp.bfloat16)
        grads.append((d_gate, d_up))
    d_cat = jnp.concatenate([g for pair in grads for g in pair], axis=1)
    w_cat = jnp.concatenate(
        [w for j in range(local_count) for w in (gate_weight[j], up_weight[j])], axis=1
    )
    token_part = dot(d_cat, w_cat, ((1,), (1,))).astype(jnp.bfloat16)
    token_rows = lax.psum_scatter(token_part, "expert", scatter_dimension=0, tiled=True)
    mixed = lax.psum_scatter(mixed_rows, "dp", scatter_dimension=1, tiled=True)
    token_grad = lax.psum_scatter(token_rows, "dp", scatter_dimension=1, tiled=True)
    gates_grad = lax.psum(
        lax.psum_scatter(gates_part, "expert", scatter_dimension=0, tiled=True), "dp"
    )

    grad_g = jnp.stack([dot(all_tokens, g, ((0,), (0,))).astype(jnp.bfloat16) for g, _ in grads])
    grad_u = jnp.stack([dot(all_tokens, u, ((0,), (0,))).astype(jnp.bfloat16) for _, u in grads])
    grad_d = jnp.stack(
        [dot(all_cotangent, s[2], ((0,), (0,))).astype(jnp.bfloat16) for s in saved]
    )
    return (mixed, token_grad, gates_grad, grad_g, grad_u, grad_d)


def expert_forward(slot_rows, w_gate, w_up, w_down):
    gate_pre = jnp.einsum("jrd,jdf->jrf", slot_rows, w_gate, preferred_element_type=jnp.float32)
    up_pre = jnp.einsum("jrd,jdf->jrf", slot_rows, w_up, preferred_element_type=jnp.float32)
    sigmoid_gate = jax.nn.sigmoid(gate_pre)
    active = gate_pre * sigmoid_gate
    hidden = (active * up_pre).astype(jnp.bfloat16)
    out_part = jnp.einsum("jrf,jdf->jrd", hidden, w_down, preferred_element_type=jnp.float32)
    return (out_part, (gate_pre, up_pre, sigmoid_gate, active, hidden))


def expert_backward(slot_rows, slot_back, saved, w_gate, w_up, w_down):
    gate_pre, up_pre, sigmoid_gate, active, hidden = saved
    dhidden = jnp.einsum("jrd,jdf->jrf", slot_back, w_down, preferred_element_type=jnp.float32)
    d_gate = (dhidden * up_pre * sigmoid_gate * (1.0 + gate_pre * (1.0 - sigmoid_gate))).astype(
        jnp.bfloat16
    )
    d_up = (dhidden * active).astype(jnp.bfloat16)
    row_part = jnp.einsum("jrf,jdf->jrd", d_gate, w_gate, preferred_element_type=jnp.float32)
    row_part = row_part + jnp.einsum("jrf,jdf->jrd", d_up, w_up, preferred_element_type=jnp.float32)
    grad_g = jnp.einsum("jrd,jrf->jdf", slot_rows, d_gate, preferred_element_type=jnp.float32)
    grad_u = jnp.einsum("jrd,jrf->jdf", slot_rows, d_up, preferred_element_type=jnp.float32)
    grad_d = jnp.einsum("jrd,jrf->jdf", slot_back, hidden, preferred_element_type=jnp.float32)
    return (row_part, (grad_g, grad_u, grad_d))


def body_slots(tokens, routing, route_gates, gate_weight, up_weight, down_weight, cotangent):
    rows_here, width = tokens.shape
    picks = routing.shape[1]
    local_count = gate_weight.shape[0]
    devices = lax.axis_size("expert")
    experts_all = local_count * devices
    capacity = 3 * rows_here * picks // (2 * experts_all)
    member = lax.axis_index("dp")
    chosen = routing.reshape(-1)
    one_hot = (chosen[:, None] == jnp.arange(experts_all, dtype=jnp.int32)[None, :]).astype(
        jnp.int32
    )
    running = jnp.cumsum(one_hot, axis=0) - one_hot
    within = jnp.sum(running * one_hot, axis=1)
    owners = chosen // local_count
    slots = chosen % local_count
    source_row = jnp.arange(rows_here * picks, dtype=jnp.int32) // picks
    flat_gates = route_gates.reshape(-1)
    x_rows = tokens[source_row]
    weighted = (flat_gates[:, None] * cotangent[source_row].astype(jnp.float32)).astype(
        jnp.bfloat16
    )
    half_cap = (capacity + 1) // 2
    mine = within // half_cap == member
    local_within = jnp.clip(within - member * half_cap, 0, half_cap - 1)
    target = jnp.where(mine, owners, devices)

    def scatter_share(values):
        buffer = jnp.zeros((local_count, devices, half_cap) + values.shape[1:], values.dtype)
        return buffer.at[slots, target, local_within].set(values, mode="drop")

    def gather_share(buffer):
        picked = buffer.at[slots, target, local_within].get(mode="fill", fill_value=0)
        return jnp.where(mine[:, None], picked, jnp.zeros((), picked.dtype))

    full_gate, full_up, full_down = (
        lax.all_gather(gate_weight, "dp", axis=2, tiled=True),
        lax.all_gather(up_weight, "dp", axis=2, tiled=True),
        lax.all_gather(down_weight, "dp", axis=2, tiled=True),
    )
    got_rows, got_back = (
        lax.all_to_all(scatter_share(x_rows), "expert", split_axis=1, concat_axis=1, tiled=True),
        lax.all_to_all(scatter_share(weighted), "expert", split_axis=1, concat_axis=1, tiled=True),
    )
    slot_rows = got_rows.reshape(local_count, devices * half_cap, width)
    slot_back = got_back.reshape(local_count, devices * half_cap, width)
    out_full, saved = expert_forward(slot_rows, full_gate, full_up, full_down)
    row_full, grads_full = expert_backward(
        slot_rows, slot_back, saved, full_gate, full_up, full_down
    )
    share_shape = (local_count, devices, half_cap, width)
    back_out, back_grad = (
        lax.all_to_all(
            out_full.astype(jnp.bfloat16).reshape(share_shape),
            "expert",
            split_axis=1,
            concat_axis=1,
            tiled=True,
        ),
        lax.all_to_all(
            row_full.astype(jnp.bfloat16).reshape(share_shape),
            "expert",
            split_axis=1,
            concat_axis=1,
            tiled=True,
        ),
    )
    expert_rows = gather_share(back_out).reshape(rows_here, picks, width)
    grad_rows = gather_share(back_grad).reshape(rows_here, picks, width)
    gate_part = jnp.einsum("td,tkd->tk", cotangent, expert_rows, preferred_element_type=jnp.float32)
    mixed_part = jnp.einsum("tk,tkd->td", route_gates, expert_rows.astype(jnp.float32))
    token_part = jnp.sum(grad_rows.astype(jnp.float32), axis=1)
    mixed_sum, token_sum = (
        lax.psum_scatter(
            mixed_part.astype(jnp.bfloat16), "dp", scatter_dimension=1, tiled=True
        ).astype(jnp.float32),
        lax.psum_scatter(
            token_part.astype(jnp.bfloat16), "dp", scatter_dimension=1, tiled=True
        ).astype(jnp.float32),
    )
    mixed = mixed_sum.astype(jnp.bfloat16)
    token_grad = token_sum.astype(jnp.bfloat16)
    grad_g, grad_u, grad_d = (
        lax.psum_scatter(
            grads_full[0].astype(jnp.bfloat16), "dp", scatter_dimension=2, tiled=True
        ).astype(jnp.float32),
        lax.psum_scatter(
            grads_full[1].astype(jnp.bfloat16), "dp", scatter_dimension=2, tiled=True
        ).astype(jnp.float32),
        lax.psum_scatter(
            grads_full[2].astype(jnp.bfloat16), "dp", scatter_dimension=2, tiled=True
        ).astype(jnp.float32),
    )
    grad_g = grad_g.astype(jnp.bfloat16)
    grad_u = grad_u.astype(jnp.bfloat16)
    grad_d = grad_d.astype(jnp.bfloat16)
    gates_grad = lax.psum(gate_part, "dp")
    return (mixed, token_grad, gates_grad, grad_g, grad_u, grad_d)


MESH = pl.DeviceIdType.MESH


class Place:
    def __init__(self, line):
        self.x = lax.axis_index("dp")
        self.e = lax.axis_index("expert")
        self.line = line
        self.z = self.e // 4
        self.y = (self.e // 2) % 2
        self.c = self.e % 2
        self.to_x = (1 - self.x, self.e)
        self.to_y = (self.x, self.e + 2 - 4 * self.y)
        self.to_core = (self.x, self.e + 1 - 2 * self.c)
        half = self.z // 2
        self.mate = self.z + 1 - 2 * (self.z % 2)
        self.inner = 2 - half
        self.outer = 3 - 3 * half
        self.between = (self.z > 0) & (self.z < line - 1)
        self.at_end = jnp.logical_not(self.between)
        self.others = (self.mate, self.inner, self.outer)

    def along(self, far):
        return (self.x, far * 4 + self.y * 2 + self.c)

    def group(self, s):
        low, high = s % 2, s // 2
        near = self.z * (1 - low) + self.mate * low
        rest = self.inner * (1 - low) + self.outer * low
        return near * (1 - high) + rest * high


def greet(p):
    barrier = pltpu.get_barrier_semaphore()
    peers = (p.to_x, p.to_y, p.to_core) + tuple(p.along(far) for far in p.others)
    for to in peers:
        pl.semaphore_signal(barrier, inc=1, device_id=to, device_id_type=MESH)
    pl.semaphore_wait(barrier, len(peers))


class Mail:
    def __init__(self, send_sem, recv_sem):
        self.send_sem, self.recv_sem, self.closing = send_sem, recv_sem, False

    def copy(self, src, dst, slot, to, send_slot=None):
        return pltpu.make_async_remote_copy(
            src_ref=src,
            dst_ref=dst,
            send_sem=self.send_sem.at[send_slot or slot],
            recv_sem=self.recv_sem.at[slot],
            device_id=to,
            device_id_type=MESH,
        )

    def send(self, src, dst, slot, to, send_slot=None):
        copy = self.copy(src, dst, slot, to, send_slot)
        if self.closing:
            copy.wait_send()
        else:
            copy.start()

    def wait(self, dst, slot, to):
        if not self.closing:
            self.copy(dst, dst, slot, to).wait_recv()

    def add(self, dst, *others):
        if not self.closing:
            total = dst[...].astype(jnp.float32)
            for other in others:
                total = total + other[...].astype(jnp.float32)
            dst[...] = total.astype(dst.dtype)


Z_IN, Y_ONE, X_TWO, X_ONE, Y_TWO, CORE, Z_OUT = range(7)
R_CORE, R_X, R_Y, R_Y2, R_X2, R_Z, R_Z_OUT = range(7, 14)
KINDS = 14


class Spread:
    def __init__(self, p, mail, pairs, routes, all_routes, own_sem):
        self.p, self.mail, self.pairs = p, mail, pairs
        self.routes, self.all_routes, self.own_sem = routes, all_routes, own_sem

    def own_copies(self, through):
        p = self.p
        found = tuple((src, dst) for src, (_, dst) in zip(through, self.pairs))
        found = found + ((self.routes, self.all_routes),)
        return [
            pltpu.make_async_copy(src, dst.at[p.z, p.y, p.c], self.own_sem.at[t])
            for t, (src, dst) in enumerate(found)
        ]

    def own_one(self):
        p, mail = self.p, self.mail
        for t, (src, dst) in enumerate(self.pairs):
            mail.send(src.at[p.x], dst.at[p.z, p.y, p.c, p.x], (t, Y_ONE, p.z), p.to_y)

    def own_to(self, far):
        p, mail = self.p, self.mail
        for t, (src, dst) in enumerate(self.pairs):
            piece = dst.at[p.z, p.y, p.c, p.x]
            mail.send(src.at[p.x], piece, (t, Z_IN, p.z), p.along(far), (t, Z_OUT, far))

    def routes_z(self):
        p, mail = self.p, self.mail
        here = self.all_routes.at[p.z, p.y, p.c]
        for far in p.others:
            mail.send(self.routes, here, (2, Z_IN, p.z), p.along(far), (2, Z_OUT, far))

    def own_two(self):
        p, mail = self.p, self.mail
        for t, (_, dst) in enumerate(self.pairs):
            piece = dst.at[p.z, 1 - p.y, p.c, p.x]
            mail.wait(piece, (t, Y_ONE, p.z), p.to_y)
            mail.send(piece, piece, (t, X_TWO, p.z), p.to_x)

    def own_three(self):
        p, mail = self.p, self.mail
        for t, (_, dst) in enumerate(self.pairs):
            mail.wait(dst.at[p.z, 1 - p.y, p.c, 1 - p.x], (t, X_TWO, p.z), p.to_x)
            mail.send(dst.at[p.z, :, p.c], dst.at[p.z, :, p.c], (t, CORE, p.z), p.to_core)

    def routes_y(self):
        p, mail, al = self.p, self.mail, self.all_routes
        for far in p.others:
            mail.wait(al.at[far, p.y, p.c], (2, Z_IN, far), p.along(far))
        mail.send(al.at[:, p.y, p.c], al.at[:, p.y, p.c], (2, Y_ONE, 0), p.to_y)

    def routes_core(self):
        p, mail, al = self.p, self.mail, self.all_routes
        mail.wait(al.at[:, 1 - p.y, p.c], (2, Y_ONE, 0), p.to_y)
        mail.send(al.at[:, :, p.c], al.at[:, :, p.c], (2, CORE, 0), p.to_core)

    def routes_end(self):
        p = self.p
        self.mail.wait(self.all_routes.at[:, :, 1 - p.c], (2, CORE, 0), p.to_core)

    def arrive(self, far, onward):
        p, mail = self.p, self.mail
        for t, (_, dst) in enumerate(self.pairs):
            piece = dst.at[far, p.y, p.c, p.x]
            mail.wait(piece, (t, Z_IN, far), p.along(far))
            if onward:
                mail.send(piece, piece, (t, Z_IN, far), p.along(p.mate))

    def one(self, t, far):
        p, mail = self.p, self.mail
        piece = self.pairs[t][1].at[far, p.y, p.c, p.x]
        mail.send(piece.at[0], piece.at[0], (t, Y_ONE, far), p.to_y)
        mail.send(piece.at[1], piece.at[1], (t, X_ONE, far), p.to_x)

    def two(self, t, far):
        p, mail = self.p, self.mail
        dst = self.pairs[t][1]
        mail.wait(dst.at[far, 1 - p.y, p.c, p.x, 0], (t, Y_ONE, far), p.to_y)
        both = dst.at[far, :, p.c, p.x, 0]
        mail.send(both, both, (t, X_TWO, far), p.to_x)
        mail.wait(dst.at[far, p.y, p.c, 1 - p.x, 1], (t, X_ONE, far), p.to_x)
        both = dst.at[far, p.y, p.c, :, 1]
        mail.send(both, both, (t, Y_TWO, far), p.to_y)

    def three(self, far):
        p, mail = self.p, self.mail
        for t, (_, dst) in enumerate(self.pairs):
            mail.wait(dst.at[far, :, p.c, 1 - p.x, 0], (t, X_TWO, far), p.to_x)
            mail.wait(dst.at[far, 1 - p.y, p.c, :, 1], (t, Y_TWO, far), p.to_y)
            mail.send(dst.at[far, :, p.c], dst.at[far, :, p.c], (t, CORE, far), p.to_core)

    def end(self, far):
        p = self.p
        for t, (_, dst) in enumerate(self.pairs):
            self.mail.wait(dst.at[far, :, 1 - p.c], (t, CORE, far), p.to_core)


class Collect:
    def __init__(self, p, mail, refs):
        vars(self).update(vars(refs))
        self.p, self.mail = p, mail
        self.cut = self.held.shape[-2] // 2

    def one(self, s, far):
        p, mail = self.p, self.mail

        @pl.when(s >= 2)
        def _():
            pl.semaphore_wait(self.free_sem, 1)

        for t in range(2):
            mail.send(self.stage.at[t], self.from_core.at[t, s % 2], (t, R_CORE, far), p.to_core)

    def merge(self, s, far):
        p, mail = self.p, self.mail
        for t in range(2):
            slot = self.from_core.at[t, s % 2]
            mail.copy(self.stage.at[t], slot, (t, R_CORE, far), p.to_core).wait()
            mail.add(self.held.at[t, far], slot)

        @pl.when(s < p.line - 2)
        def _():
            pl.semaphore_signal(
                self.free_sem, inc=1, device_id=p.to_core, device_id_type=MESH
            )

    def two(self, far):
        p, mail, held, cut = self.p, self.mail, self.held, self.cut
        for t in range(2):
            mail.send(
                held.at[t, far, :, 1 - p.x, :cut], self.from_x.at[t, far], (t, R_X, far), p.to_x
            )
            mail.send(
                held.at[t, far, 1 - p.y, :, cut:], self.from_y.at[t, far], (t, R_Y, far), p.to_y
            )

    def three(self, far):
        p, mail, held, cut = self.p, self.mail, self.held, self.cut
        for t in range(2):
            mail.wait(self.from_x.at[t, far], (t, R_X, far), p.to_x)
            mail.add(held.at[t, far, :, p.x, :cut], self.from_x.at[t, far])
            mail.send(
                held.at[t, far, 1 - p.y, p.x, :cut], self.from_y2.at[t, far], (t, R_Y2, far), p.to_y
            )
            mail.wait(self.from_y.at[t, far], (t, R_Y, far), p.to_y)
            mail.add(held.at[t, far, p.y, :, cut:], self.from_y.at[t, far])
            mail.send(
                held.at[t, far, p.y, 1 - p.x, cut:], self.from_x2.at[t, far], (t, R_X2, far), p.to_x
            )

    def joined(self, t, far):
        p, mail, held, cut = self.p, self.mail, self.held, self.cut
        mail.wait(self.from_y2.at[t, far], (t, R_Y2, far), p.to_y)
        mail.add(held.at[t, far, p.y, p.x, :cut], self.from_y2.at[t, far])
        mail.wait(self.from_x2.at[t, far], (t, R_X2, far), p.to_x)
        mail.add(held.at[t, far, p.y, p.x, cut:], self.from_x2.at[t, far])

    def pass_on(self, t, far, mine, arrived):
        p = self.p
        self.mail.send(mine, arrived.at[p.z], (t, R_Z, p.z), p.along(far), (t, R_Z_OUT, far))

    def last(self, t, mine, arrived, dst):
        p, mail = self.p, self.mail
        total = mine[...].astype(jnp.float32)
        for far in p.others:
            mail.wait(arrived.at[far], (t, R_Z, far), p.along(far))
            total = total + arrived[far].astype(jnp.float32)
        dst[...] = total.astype(dst.dtype)

    def four(self, far):
        p = self.p
        for t in range(2):
            self.joined(t, far)
            self.pass_on(t, far, self.held.at[t, far, p.y, p.x], self.from_z.at[t])

    def pair_on(self, far):
        self.pass_on(2, far, self.pair_sum.at[far], self.pair_z)

    def four_own(self, mixed, token_grad, gates_grad):
        p = self.p
        for t, dst in ((0, mixed), (1, token_grad)):
            self.joined(t, p.z)
            self.last(t, self.held.at[t, p.z, p.y, p.x], self.from_z.at[t], dst)
        self.last(2, self.pair_sum.at[p.z], self.pair_z, gates_grad)

    def pair_one(self):
        self.mail.send(self.pair_stage, self.pair_core, (2, R_CORE, 0), self.p.to_core)

    def pair_two(self):
        p, mail = self.p, self.mail
        mail.wait(self.pair_core, (2, R_CORE, 0), p.to_core)
        mail.add(self.held_pair, self.pair_core)
        mail.send(self.held_pair.at[:, 1 - p.y], self.pair_y, (2, R_Y, 0), p.to_y)

    def pair_three(self):
        p, mail = self.p, self.mail
        mail.wait(self.pair_y, (2, R_Y, 0), p.to_y)
        mail.add(self.held_pair.at[:, p.y], self.pair_y)
        mail.send(self.held_pair.at[:, p.y], self.pair_x, (2, R_X, 0), p.to_x)

    def pair_four(self):
        p = self.p
        self.mail.wait(self.pair_x, (2, R_X, 0), p.to_x)
        self.pair_sum[...] = self.held_pair[:, p.y] + self.pair_x[...]


def experts(cap, p, s, far, tok, cot, routes, w_gate, w_up, w_down, held, stage, held_pair,
            pair_stage, x_rows, c_rows, d_both, w_hidden, pick):
    count, width, hidden_units = w_gate.shape
    blocks = 4
    group = blocks * cap
    rows = routes.shape[-1]
    picks = routes.shape[-2] // 2
    first = p.e * count
    start = pl.multiple_of(s * group, group)
    lower = (
        lax.broadcasted_iota(jnp.int32, (rows, rows), 0)
        < lax.broadcasted_iota(jnp.int32, (rows, rows), 1)
    ).astype(jnp.bfloat16)
    slot = lax.broadcasted_iota(jnp.int32, (cap, rows), 0).astype(jnp.float32)
    place = [(b // 2, (p.c + b % 2) % 2) for b in range(blocks)]

    hits, gate_cols = [], []
    for b, (yy, cc) in enumerate(place):
        rt = routes[far, yy, cc, :picks]
        gt = routes[far, yy, cc, picks:]
        hit_b, gate_b = [], []
        for j in range(count):
            hit = (rt == (first + j).astype(jnp.float32)).astype(jnp.float32)
            named = jnp.sum(hit, axis=0, keepdims=True)
            gate = jnp.sum(hit * gt, axis=0, keepdims=True)
            named8 = jnp.broadcast_to(named, (8, rows)).astype(jnp.bfloat16)
            rank = jnp.dot(named8, lower, preferred_element_type=jnp.float32)[:1]
            rank = jnp.where(named > 0.5, rank, -1.0)
            chosen = (slot == rank).astype(jnp.float32)
            gate_b.append(jnp.sum(chosen * gate, axis=1, keepdims=True))
            hit_b.append(hit)
            pick[b, j * cap:(j + 1) * cap] = chosen.astype(jnp.bfloat16)
        hits.append(hit_b)
        gate_cols.append(gate_b)

    for b, (yy, cc) in enumerate(place):
        for src, dst in ((tok, x_rows), (cot, c_rows)):
            block = src[yy, cc].reshape(rows, width)
            got = jnp.dot(pick[b], block, preferred_element_type=jnp.float32)
            for j in range(count):
                at = pl.ds(pl.multiple_of(start + b * cap, 16), cap)
                dst[j, at] = got[j * cap:(j + 1) * cap].astype(jnp.bfloat16)

    at = pl.ds(start, group)
    pairs = []
    for j in range(count):
        gate_pre = jnp.dot(x_rows[j, at], w_gate[j], preferred_element_type=jnp.float32)
        up_pre = jnp.dot(x_rows[j, at], w_up[j], preferred_element_type=jnp.float32)
        raw = jnp.dot(c_rows[j, at], w_down[j], preferred_element_type=jnp.float32)
        gate = jnp.concatenate([gate_cols[b][j] for b in range(blocks)], axis=0)
        sig = jax.nn.sigmoid(gate_pre)
        active = gate_pre * sig
        hidden = active * up_pre
        back = gate * raw
        wh = (gate * hidden).astype(jnp.bfloat16)
        dg = (back * up_pre * sig * (1.0 + gate_pre * (1.0 - sig))).astype(jnp.bfloat16)
        du = (back * active).astype(jnp.bfloat16)
        w_hidden[j, at] = wh
        d_both[j, at, :hidden_units] = dg
        d_both[j, at, hidden_units:] = du
        pairs.append(jnp.sum(raw * hidden, axis=1, keepdims=True))
        nt = (((1,), (1,)), ((), ()))
        out = lax.dot_general(wh, w_down[j], nt, preferred_element_type=jnp.float32)
        row = lax.dot_general(dg, w_gate[j], nt, preferred_element_type=jnp.float32)
        row = row + lax.dot_general(du, w_up[j], nt, preferred_element_type=jnp.float32)
        for b, (yy, cc) in enumerate(place):
            for q in range(0, cap, 16):
                piece, low = divmod(j * cap + q, tok.shape[-2])
                to = (yy, cc, piece // 2, piece % 2, slice(low, low + 16))
                tok[to] = out[b * cap + q:b * cap + q + 16].astype(jnp.bfloat16)
                cot[to] = row[b * cap + q:b * cap + q + 16].astype(jnp.bfloat16)

    half = width // 2
    for b, (yy, cc) in enumerate(place):
        total = jnp.zeros((picks, rows), jnp.float32)
        for j in range(count):
            chosen = pick[b, j * cap:(j + 1) * cap].astype(jnp.float32)
            line = jnp.sum(chosen * pairs[j][b * cap:(b + 1) * cap], axis=0, keepdims=True)
            total = total + hits[b][j] * line
        if b % 2 == 0:
            held_pair[far, yy] = total
        else:
            pair_stage[far, yy] = total
        tn = (((0,), (0,)), ((), ()))
        for t, src in enumerate((tok, cot)):
            found = src[yy, cc].reshape(rows, width)
            for f in range(2):
                value = lax.dot_general(
                    pick[b], found[:count * cap, f * half:(f + 1) * half], tn,
                    preferred_element_type=jnp.float32,
                ).astype(jnp.bfloat16)
                if b % 2 == 0:
                    held[t, far, yy, f] = value
                else:
                    stage[t, yy, f] = value


def weight_grads(j, m, rows, d_rows, *grads):
    width, hidden_units = grads[0].shape[-2:]
    chunk = width // 8

    def part(k, carry):
        at = pl.ds(pl.multiple_of(k * chunk, chunk), chunk)
        value = lax.dot_general(
            rows[j, :, at], d_rows[j], (((0,), (0,)), ((), ())),
            preferred_element_type=jnp.float32,
        ).astype(jnp.bfloat16)
        for i, grad in enumerate(grads):
            grad[j, at] = value[:, i * hidden_units:(i + 1) * hidden_units]
        return carry

    lax.fori_loop(2 * m, 2 * m + 2, part, 0)


def layer_kernel(line, cap, names, *refs):
    r = types.SimpleNamespace(**dict(zip(names, refs)))
    p = Place(line)
    mail = Mail(r.send_sem, r.recv_sem)
    pairs = ((r.tok, r.all_tok), (r.cot, r.all_cot))
    spread = Spread(p, mail, pairs, r.routes, r.all_routes, r.own_sem)
    collect = Collect(p, mail, r)
    through = (r.tok_in.at[0, 0], r.cot_in.at[0, 0])
    taken = [
        pltpu.make_async_copy(src, dst, r.own_sem.at[t])
        for t, (src, dst) in enumerate(zip((r.tok, r.cot), through))
    ]
    own = spread.own_copies(through)
    for copy in taken:
        copy.start()
    weights = [
        pltpu.make_async_copy(src, dst, r.load_sem.at[i])
        for i, (src, dst) in enumerate(
            ((r.w_gate, r.w_gate_in), (r.w_up, r.w_up_in), (r.w_down, r.w_down_in))
        )
    ]
    greet(p)
    spread.own_one()
    spread.own_to(p.mate)
    spread.routes_z()
    spread.own_to(p.inner)
    for copy in taken:
        copy.wait()
    for copy in own + weights:
        copy.start()

    def first_phase():
        spread.own_two()
        spread.arrive(p.mate, False)
        for t in range(2):
            spread.one(t, p.mate)
        spread.two(0, p.mate)
        if not mail.closing:
            for copy in own:
                copy.wait()
        spread.own_three()
        pl.when(p.between)(functools.partial(spread.arrive, p.inner, True))
        spread.routes_y()
        spread.two(1, p.mate)
        spread.routes_core()

    def second_phase():
        pl.when(p.at_end)(functools.partial(spread.arrive, p.inner, False))
        for t in range(2):
            spread.one(t, p.inner)
        pl.when(p.between)(functools.partial(spread.arrive, p.outer, True))
        spread.three(p.mate)
        for t in range(2):
            spread.two(t, p.inner)

    def third_phase():
        pl.when(p.at_end)(functools.partial(spread.arrive, p.outer, False))
        for t in range(2):
            spread.one(t, p.outer)
        spread.three(p.inner)
        for t in range(2):
            spread.two(t, p.outer)

    def fourth_phase():
        spread.three(p.outer)
        collect.two(p.mate)

    first_phase()
    for copy in weights:
        copy.wait()
    spread.routes_end()

    def grads_of(j, m):
        at = pl.ds(m * (r.w_gate.shape[1] // 4), r.w_gate.shape[1] // 4)
        return [
            pltpu.make_async_copy(src.at[j, at], dst.at[j, at], r.save_sem.at[i, j, m])
            for i, (src, dst) in enumerate(
                ((r.w_gate_in, r.gate_grad), (r.w_up_in, r.up_grad), (r.w_down_in, r.down_grad))
            )
        ]

    def gate_up_grads(j, m):
        weight_grads(j, m, r.x_rows, r.d_both, r.w_gate_in, r.w_up_in)
        for copy in grads_of(j, m)[:2]:
            copy.start()

    def down_grads(j, m):
        weight_grads(j, m, r.c_rows, r.w_hidden, r.w_down_in)
        grads_of(j, m)[2].start()

    def step(s, carry):
        far = p.group(s)
        pl.when(s == 1)(second_phase)
        pl.when(s == 2)(third_phase)
        pl.when(s == 3)(fourth_phase)
        spread.end(far)
        loads = [
            pltpu.make_async_copy(src.at[far], dst, r.load_sem.at[i])
            for i, (src, dst) in enumerate(((r.all_tok, r.tok_in), (r.all_cot, r.cot_in)))
        ]
        for copy in loads:
            copy.start()

        @pl.when(s > 0)
        def _():
            collect.merge(s - 1, p.group(s - 1))

        @pl.when(s == 3)
        def _():
            collect.two(p.inner)

        for copy in loads:
            copy.wait()
        experts(
            cap, p, s, far, r.tok_in, r.cot_in, r.all_routes, r.w_gate_in,
            r.w_up_in, r.w_down_in, r.held, r.stage, r.held_pair, r.pair_stage,
            r.x_rows, r.c_rows, r.d_both, r.w_hidden, r.pick,
        )
        collect.one(s, far)
        return carry

    lax.fori_loop(0, line, step, 0)
    count = r.w_gate.shape[0]
    work = [
        functools.partial(f, j, m)
        for j in range(count) for m in range(4) for f in (gate_up_grads, down_grads)
    ]

    whole = len(work)

    def some_work(parts):
        for piece in work[:parts * whole // 16]:
            piece()
        del work[:parts * whole // 16]

    collect.pair_one()
    collect.merge(line - 1, p.outer)
    collect.two(p.outer)
    collect.three(p.inner)
    collect.three(p.mate)
    collect.two(p.z)
    collect.pair_two()
    some_work(4)
    collect.four(p.inner)
    collect.four(p.mate)
    collect.three(p.outer)
    collect.pair_three()
    collect.four(p.outer)
    some_work(2)
    collect.three(p.z)
    collect.pair_four()
    for far in p.others:
        collect.pair_on(far)
    some_work(16)
    collect.four_own(r.mixed, r.token_grad, r.gates_grad)
    for j in range(count):
        for m in range(4):
            for copy in grads_of(j, m):
                copy.wait()

    mail.closing = True
    spread.own_one()
    spread.own_to(p.mate)
    spread.routes_z()
    spread.own_to(p.inner)
    first_phase()
    second_phase()
    third_phase()
    fourth_phase()
    collect.pair_one()
    for far in (p.inner, p.outer, p.z,):
        collect.two(far)
    for far in (p.mate, p.inner, p.outer, p.z,):
        collect.three(far)
    collect.pair_two()
    collect.pair_three()
    for far in p.others:
        for t in range(2):
            collect.pass_on(t, far, r.held.at[t, far, p.y, p.x], r.from_z.at[t])
        collect.pair_on(far)


def body_lines(tokens, routing, route_gates, gate_weight, up_weight, down_weight, cotangent):
    rows, width = tokens.shape
    picks = routing.shape[1]
    count, _, hidden_units = gate_weight.shape
    devices = lax.axis_size("expert")
    line = devices // 4
    cap = 3 * rows * picks // (2 * count * devices)
    half, cut = width // 2, rows // 2
    slots = line * 4 * cap
    bf16, f32 = jnp.bfloat16, jnp.float32
    anywhere = pl.BlockSpec(memory_space=pl.ANY)
    in_vmem = pl.BlockSpec(memory_space=pltpu.VMEM)

    routes = jnp.concatenate([routing.astype(f32).T, route_gates.T], axis=0)
    quarters = (2, 2, rows // 4, width)
    inputs = dict(
        tok=tokens.reshape(quarters),
        cot=cotangent.reshape(quarters),
        routes=routes,
        w_gate=gate_weight,
        w_up=up_weight,
        w_down=down_weight,
    )
    shape = jax.ShapeDtypeStruct
    outs = dict(
        mixed=(shape((rows, half), bf16), in_vmem),
        token_grad=(shape((rows, half), bf16), in_vmem),
        gates_grad=(shape((picks, rows), f32), in_vmem),
        gate_grad=(shape(gate_weight.shape, bf16), anywhere),
        up_grad=(shape(gate_weight.shape, bf16), anywhere),
        down_grad=(shape(gate_weight.shape, bf16), anywhere),
        all_tok=(shape((line, 2, 2) + quarters, bf16), anywhere),
        all_cot=(shape((line, 2, 2) + quarters, bf16), anywhere),
    )
    weight = pltpu.VMEM((count, width, hidden_units), bf16)
    scratch = dict(
        all_routes=pltpu.VMEM((line, 2, 2, 2 * picks, rows), f32),
        w_gate_in=weight,
        w_up_in=weight,
        w_down_in=weight,
        tok_in=pltpu.VMEM((2, 2) + quarters, bf16),
        cot_in=pltpu.VMEM((2, 2) + quarters, bf16),
        x_rows=pltpu.VMEM((count, slots, width), bf16),
        c_rows=pltpu.VMEM((count, slots, width), bf16),
        d_both=pltpu.VMEM((count, slots, 2 * hidden_units), bf16),
        w_hidden=pltpu.VMEM((count, slots, hidden_units), bf16),
        pick=pltpu.VMEM((4, count * cap, rows), bf16),
        held=pltpu.VMEM((2, line, 2, 2, rows, half), bf16),
        stage=pltpu.VMEM((2, 2, 2, rows, half), bf16),
        from_core=pltpu.VMEM((2, 2, 2, 2, rows, half), bf16),
        from_x=pltpu.VMEM((2, line, 2, cut, half), bf16),
        from_y=pltpu.VMEM((2, line, 2, cut, half), bf16),
        from_y2=pltpu.VMEM((2, line, cut, half), bf16),
        from_x2=pltpu.VMEM((2, line, cut, half), bf16),
        from_z=pltpu.VMEM((2, line, rows, half), bf16),
        held_pair=pltpu.VMEM((line, 2, picks, rows), f32),
        pair_stage=pltpu.VMEM((line, 2, picks, rows), f32),
        pair_core=pltpu.VMEM((line, 2, picks, rows), f32),
        pair_y=pltpu.VMEM((line, picks, rows), f32),
        pair_x=pltpu.VMEM((line, picks, rows), f32),
        pair_sum=pltpu.VMEM((line, picks, rows), f32),
        pair_z=pltpu.VMEM((line, picks, rows), f32),
        send_sem=pltpu.SemaphoreType.DMA((3, KINDS, line)),
        recv_sem=pltpu.SemaphoreType.DMA((3, KINDS, line)),
        free_sem=pltpu.SemaphoreType.REGULAR,
        own_sem=pltpu.SemaphoreType.DMA((3,)),
        load_sem=pltpu.SemaphoreType.DMA((3,)),
        save_sem=pltpu.SemaphoreType.DMA((3, count, 4)),
    )
    names = list(inputs) + list(outs) + list(scratch)
    got = pl.pallas_call(
        functools.partial(layer_kernel, line, cap, names),
        out_shape=[v[0] for v in outs.values()],
        in_specs=[anywhere] * len(inputs),
        out_specs=[v[1] for v in outs.values()],
        scratch_shapes=list(scratch.values()),
        compiler_params=pltpu.CompilerParams(
            collective_id=0, has_side_effects=True, vmem_limit_bytes=64 << 20
        ),
        name="layer",
    )(*inputs.values())
    got = types.SimpleNamespace(**dict(zip(outs, got)))

    return (
        got.mixed,
        got.token_grad,
        got.gates_grad.T,
        got.gate_grad,
        got.up_grad,
        got.down_grad,
    )


def body(tokens, *rest):
    devices = lax.axis_size("expert")
    if lax.axis_size("dp") == 2 and devices == 16:
        return body_lines(tokens, *rest)
    held = 8 * tokens.size * tokens.dtype.itemsize * devices
    return (body_whole if held < 1 << 27 else body_slots)(tokens, *rest)


def solution(mesh):
    in_specs = (
        P("expert", None),
        P("expert", None),
        P("expert", None),
        P("expert", None, "dp"),
        P("expert", None, "dp"),
        P("expert", None, "dp"),
        P("expert", None),
    )
    out_specs = (
        P("expert", "dp"),
        P("expert", "dp"),
        P("expert", None),
        P("expert", None, "dp"),
        P("expert", None, "dp"),
        P("expert", None, "dp"),
    )
    return jax.shard_map(body, mesh=mesh, in_specs=in_specs, out_specs=out_specs, check_vma=False)
```
